32 devices in a mesh: shard: 4 (over y, core), ctx: 4 (over z), tensor: 2 (over x).
Axes of the slice: x: 2, y: 2, z: 4, core: 2. Of those that a mesh axis runs over, the one named last changes fastest.
Arguments:
- layer_input: bfloat16 [4, 2048, 768], P('shard', 'ctx'), may hold values from -6 to 6
- segments: int32 [4, 2048], P('shard'), may hold values from 0 to 2, as said below
- w_qkv: bfloat16 [768, 3, 768], P(('shard', 'ctx'), None, 'tensor'), may hold values from -0.21875 to 0.21875
- b_qv: bfloat16 [2, 768], P(None, 'tensor'), may hold values from -2 to 2
- w_out: bfloat16 [768, 768], P(('shard', 'ctx'), 'tensor'), may hold values from -4 to 4
- b_out: bfloat16 [768], replicated, may hold values from -2 to 2
- ln1_gain: bfloat16 [768], replicated, may hold values from 0.25 to 1.75
- ln1_bias: bfloat16 [768], replicated, may hold values from -2 to 2
- w_up: bfloat16 [768, 3072], P(('shard', 'ctx'), 'tensor'), may hold values from -0.21875 to 0.21875
- b_up: bfloat16 [3072], P('tensor'), may hold values from -2 to 2
- w_down: bfloat16 [768, 3072], P(('shard', 'ctx'), 'tensor'), may hold values from -0.109375 to 0.109375
- b_down: bfloat16 [768], replicated, may hold values from -2 to 2
- ln2_gain: bfloat16 [768], replicated, may hold values from 0.25 to 1.75
- ln2_bias: bfloat16 [768], replicated, may hold values from -2 to 2
- cotangent: bfloat16 [4, 2048, 768], P('shard', 'ctx'), may hold values from -6 to 6
Outputs:
- layer_output: bfloat16 [4, 2048, 768], P('shard', 'ctx')
- grad_input: float32 [4, 2048, 768], P('shard', 'ctx')
- grad_w_qkv: float32 [768, 3, 768], P(('shard', 'ctx'), None, 'tensor')
- grad_b_qv: float32 [2, 768], P(None, 'tensor')
- grad_w_out: float32 [768, 768], P(('shard', 'ctx'), 'tensor')
- grad_b_out: float32 [768], replicated
- grad_ln1_gain: float32 [768], replicated
- grad_ln1_bias: float32 [768], replicated
- grad_w_up: float32 [768, 3072], P(('shard', 'ctx'), 'tensor')
- grad_b_up: float32 [3072], P('tensor')
- grad_w_down: float32 [768, 3072], P(('shard', 'ctx'), 'tensor')
- grad_b_down: float32 [768], replicated
- grad_ln2_gain: float32 [768], replicated
- grad_ln2_bias: float32 [768], replicated
The draws below stay inside these ranges and needn't reach their ends.
Inputs may be any that keep to these rules, and one draw needn't show every extreme that they name: Each packed row has exactly three segments numbered 0, 1, 2, never falling along the row; segment 1 starts within the first 512 positions and ends within the last 512 positions of the row.
All inputs are finite; a program needn't handle non-finite values.
Results may differ from the reference program's by a relative error of at most 0.02.
Values may be sent and summed in bfloat16 or wider, within the bound.
No kernel may reach another device: no remote copies, remote signals or barrier semaphores. Data moves between devices by JAX's collectives and lax.ppermute only.
A program may use at most 128 MiB of HBM per device.

```python
import jax
import jax.numpy as jnp
from jax import lax

D = 768
H = 12
HD = 64
FF = 3072
TOK_DEV = 512
GROUPS = 4
GROUP_LEN = 2048


def draw_segments(key, part):
    first_key, second_key = jax.random.split(jax.random.fold_in(key, 17))
    starts = jax.random.randint(first_key, (GROUPS, 1), 1, TOK_DEV)
    endings = jax.random.randint(second_key, (GROUPS, 1), GROUP_LEN - TOK_DEV, GROUP_LEN - 1)
    places = jnp.arange(GROUP_LEN, dtype=jnp.int32)[None, :]
    return (places >= starts).astype(jnp.int32) + (places >= endings).astype(jnp.int32)


def block_scale(own_key, dims, pieces, smallest, largest):
    factor_of, own = 1.0, jax.random.fold_in(own_key, 6)
    for axis_at, shards_of in pieces:
        steps = jnp.exp(jax.random.uniform(jax.random.fold_in(own, axis_at), (shards_of,), jnp.float32, smallest / len(pieces), largest / len(pieces)))
        factor_of = factor_of * jnp.repeat(steps, dims[axis_at] // shards_of).reshape([-1 if axis == axis_at else 1 for axis in range(len(dims))])
    return factor_of


def bell_draw(key, dims, deviation, most, pieces=(), kind=jnp.bfloat16):
    drawn = jax.random.normal(key, dims, jnp.float32) * deviation
    if len(pieces) > 0:
        drawn = block_scale(key, dims, pieces, -0.22, 0.18) * drawn
    return jnp.clip(drawn, min=-most, max=most).astype(kind)


def setup_inputs(seed: int = 0) -> dict:
    streams_of = jax.random.split(jax.random.key(seed), 16)
    layer_input = bell_draw(streams_of[0], (GROUPS, GROUP_LEN, D), 1.0, 6.0, ((0, 4), (1, 4)))
    segments = draw_segments(jax.random.fold_in(streams_of[15], 71), 0)
    w_qkv = bell_draw(streams_of[2], (D, 3, D), D ** -0.5, 0.21875, ((0, 16), (2, 2)))
    b_qv = bell_draw(streams_of[3], (2, D), 0.3, 2.0, ((1, 2),))
    w_out = bell_draw(streams_of[4], (D, D), 1.0, 4.0, ((0, 16), (1, 2)))
    b_out = bell_draw(streams_of[5], (D,), 0.3, 2.0)
    ln1_gain = jnp.clip(1.0 + 0.15 * jax.random.normal(streams_of[6], (D,), jnp.float32), 0.25, 1.75).astype(jnp.bfloat16)
    ln1_bias = bell_draw(streams_of[7], (D,), 0.3, 2.0)
    w_up = bell_draw(streams_of[8], (D, FF), D ** -0.5, 0.21875, ((0, 16), (1, 2)))
    b_up = bell_draw(streams_of[9], (FF,), 0.3, 2.0, ((0, 2),))
    w_down = bell_draw(streams_of[10], (D, FF), FF ** -0.5, 0.109375, ((0, 16), (1, 2)))
    b_down = bell_draw(streams_of[11], (D,), 0.3, 2.0)
    ln2_gain = jnp.clip(1.0 + 0.15 * jax.random.normal(streams_of[12], (D,), jnp.float32), 0.25, 1.75).astype(jnp.bfloat16)
    ln2_bias = bell_draw(streams_of[13], (D,), 0.3, 2.0)
    cotangent = bell_draw(streams_of[14], (GROUPS, GROUP_LEN, D), 1.0, 6.0, ((0, 4), (1, 4)))
    return dict(layer_input=layer_input, segments=segments, w_qkv=w_qkv, b_qv=b_qv, w_out=w_out, b_out=b_out, ln1_gain=ln1_gain, ln1_bias=ln1_bias, w_up=w_up, b_up=b_up, w_down=w_down, b_down=b_down, ln2_gain=ln2_gain, ln2_bias=ln2_bias, cotangent=cotangent)


highest = lax.Precision.HIGHEST
neg_large = -1e+30

@jax.custom_vjp
def low(v):
    return lax.optimization_barrier(v.astype(jnp.bfloat16)).astype(jnp.float32)

@jax.custom_vjp
def low_back(v):
    return v

def low_keep(v):
    return (low(v), None)

def low_pass(kept, grad):
    return (grad,)

def back_keep(v):
    return (v, None)

def back_low(kept, grad):
    return (low(grad),)
low.defvjp(low_keep, low_pass)
low_back.defvjp(back_keep, back_low)

def normed(summed, gain, bias):
    centred = summed - lax.optimization_barrier(jnp.mean(summed, -1, keepdims=True))
    scaling = lax.rsqrt(lax.optimization_barrier(jnp.mean(centred * centred, -1, keepdims=True)) + 1e-05)
    return centred * scaling * gain + bias

def split_heads(matrix):
    return matrix.reshape(matrix.shape[0], H, HD).transpose(1, 0, 2)

def attend(query_heads, key_heads, value_heads, seg_query, seg_keys):
    scores = low_back(0.125 * jnp.einsum('hqd,hkd->hqk', query_heads, key_heads, precision=highest))
    scores = jnp.where((seg_query[:, None] == seg_keys[None, :])[None], scores, neg_large)
    probs = low(jnp.exp(scores - jax.nn.logsumexp(scores, axis=-1, keepdims=True)))
    return jnp.einsum('hqk,hkd->hqd', probs, value_heads, precision=highest)

def layer(inputs, seg_row, w_qkv, b_qv, w_out, b_out, gain_first, bias_first, w_up, b_up, w_down, b_down, gain_second, bias_second):
    length = inputs.shape[0]
    rounded = low(inputs)
    projected = jnp.einsum('td,dwe->wte', rounded, w_qkv, precision=highest)
    queries = low(low_back(projected[0]) + b_qv[0])
    key_rows = low(low_back(projected[1]))
    value_rows = low(low_back(projected[2]) + b_qv[1])
    block_rows = min(512, length)
    count_blocks = length // block_rows
    query_blocks = split_heads(queries).reshape(H, count_blocks, block_rows, HD).transpose(1, 0, 2, 3)
    seg_blocks = seg_row.reshape(count_blocks, block_rows)
    key_heads = split_heads(key_rows)
    value_heads = split_heads(value_rows)

    def one_block(element):
        return attend(element[0], key_heads, value_heads, element[1], seg_row)
    mixed = lax.map(jax.checkpoint(one_block), (query_blocks, seg_blocks))
    attended = low(low_back(mixed.transpose(0, 2, 1, 3).reshape(length, H * HD)))
    branch = low_back(jnp.dot(attended, w_out.T, precision=highest)) + b_out
    hidden = normed(inputs + branch, gain_first, bias_first)
    pre_act = low_back(jnp.dot(low(hidden), w_up, precision=highest)) + b_up
    activated = low(jax.nn.gelu(pre_act, approximate=False))
    second_branch = low_back(jnp.dot(activated, w_down.T, precision=highest)) + b_down
    return normed(hidden + second_branch, gain_second, bias_second)

def reference(layer_input, segments, w_qkv, b_qv, w_out, b_out, ln1_gain, ln1_bias, w_up, b_up, w_down, b_down, ln2_gain, ln2_bias, cotangent):
    params = tuple((weight.astype(jnp.float32) for weight in (w_qkv, b_qv, w_out, b_out, ln1_gain, ln1_bias, w_up, b_up, w_down, b_down, ln2_gain, ln2_bias)))

    def group(totals, element):
        rows_in, seg_row, cot_row = element

        def forward(inputs, *weights):
            return layer(inputs, seg_row, *weights)
        result, pullback = jax.vjp(forward, rows_in.astype(jnp.float32), *params)
        grads = pullback(cot_row.astype(jnp.float32))
        totals = tuple((summed + update for summed, update in zip(totals, grads[1:])))
        return (totals, (result.astype(jnp.bfloat16), grads[0]))
    zeros = tuple((jnp.zeros_like(weight) for weight in params))
    totals, (outputs, grad_inputs) = lax.scan(group, zeros, (layer_input, segments, cotangent))
    return (outputs, grad_inputs, totals[0], totals[1], totals[2], totals[3], totals[4], totals[5], totals[6], totals[7], totals[8], totals[9], totals[10], totals[11])
```

```python
import math

import jax
import jax.numpy as jnp
from jax import lax
from jax.experimental import pallas as pl
from jax.experimental.pallas import tpu as pltpu
from jax.sharding import Mesh
from jax.sharding import PartitionSpec as P

HD = 64
LANES = 128
BF = jnp.bfloat16
F32 = jnp.float32
NT = (((1,), (1,)), ((), ()))
NN = (((1,), (0,)), ((), ()))
EVERY = ("y", "core", "ctx", "tensor")
SWAP = ((0, 1), (1, 0))


def mm(a, b, dims=NN):
    return lax.dot_general(a, b, dims, preferred_element_type=F32)


def params(mib):
    return pltpu.CompilerParams(vmem_limit_bytes=mib << 20)


def anywhere():
    return pl.BlockSpec(memory_space=pl.ANY)


def whole(shape):
    return pl.BlockSpec(shape, lambda *_: (0,) * len(shape))


def scalars():
    return pl.BlockSpec(memory_space=pltpu.SMEM)


def owner_of(ids, piece, ctx):
    rc, ry, rx, rz = piece
    y = (ids[0] + ry) % 2
    core = (ids[1] + rc) % 2
    place = (ids[2] + (ctx - rz)) % ctx
    return (y * 2 + core) * ctx + place, (ids[3] + rx) % 2


def piece_copies(ids, refs, layout, full, sem, ctx, rows, width, back=False, base=0):
    copies = []
    for ref, pieces, at in zip(refs, layout, range(len(refs))):
        for index, piece in pieces:
            block, half = owner_of(ids, piece, ctx)
            row = pl.multiple_of(block * rows, 16)
            column = pl.multiple_of(half * width, LANES)
            if len(full.shape) == 3:
                there = full.at[:, pl.ds(row, rows), pl.ds(column, width)]
            else:
                there = full.at[pl.ds(row, rows), pl.ds(column, width)]
            here = ref.at[index]
            source, target = (there, here) if back else (here, there)
            copies.append(pltpu.make_async_copy(source, target, sem.at[base + len(copies)]))
    return copies


def prepare_kernel(ctx, rows, width, layout, n, heads, scale, ids, xt, bq, *rest):
    pieces, (weights, queries, sem) = rest[:n], rest[n:]
    copies = piece_copies(ids, pieces, layout, weights, sem, ctx, rows, width)
    for copy in copies:
        copy.start()
    for copy in copies:
        copy.wait()
    tokens = xt.shape[0]
    lane = lax.broadcasted_iota(jnp.int32, (tokens, LANES), 1)
    projected = mm(xt[...], weights[0]) + bq[...]
    projected = (projected.astype(BF).astype(F32) * scale)
    for pair in range(heads // 2):
        two = projected[:, pair * LANES : (pair + 1) * LANES]
        even = jnp.where(lane < HD, two, 0.0).astype(BF)
        odd = jnp.where(lane >= HD, two, 0.0).astype(BF)
        queries[pair] = jnp.concatenate([even, odd], 0)


def attend_kernel(first, xa, xb, wk, wv, bv, queries, qmark, kmark, *rest):
    if first:
        keys, values, keys_t, top_out, sums_out = rest
    else:
        top_in, sums_in, keys, values, keys_t, top_out, sums_out = rest
    x = jnp.concatenate([xa[...], xb[...]], 0)
    k4 = mm(x, wk[...]).astype(BF)
    v4 = mm(x, wv[...]) + bv[...]
    keys[...] = k4
    values[...] = v4.astype(BF)
    keys_t[...] = k4.T
    v4t = v4.T.astype(BF)
    ones = jnp.ones((16, x.shape[0]), BF)
    for j in range(2):
        span = slice(j * LANES, (j + 1) * LANES)
        kk = jnp.concatenate([k4[:, span], kmark[...]], 1)
        qq = jnp.concatenate([queries[j], qmark[...]], 1)
        scores = mm(kk, qq, NT)
        top = jnp.max(scores, 0, keepdims=True)
        if not first:
            top = jnp.maximum(top, top_in[j])
        probs = jnp.exp(scores - top).astype(BF)
        sums = mm(jnp.concatenate([v4t[span], ones], 0), probs)
        if not first:
            sums = sums + sums_in[j] * jnp.exp(top_in[j] - top)
        top_out[j] = top
        sums_out[j] = sums


def normed(z, eps=1e-05):
    centred = z - jnp.mean(z, -1, keepdims=True)
    factor = lax.rsqrt(jnp.mean(centred * centred, -1, keepdims=True) + eps)
    return centred * factor, factor


def norm_back(e, n, factor, gain):
    scaled = e * gain
    return factor * (
        scaled - jnp.mean(scaled, -1, keepdims=True) - n * jnp.mean(scaled * n, -1, keepdims=True)
    )


def total(v):
    return jnp.sum(v, 0, keepdims=True)


def middle_kernel(ctx, rows, lay_up, lay_down, lay_out, n_up, n_down, heads, ids, sums, top, xt, cot, vec, b_up, *rest):
    ups, rest = rest[:n_up], rest[n_up:]
    downs, rest = rest[:n_down], rest[n_down:]
    (
        out_ref, dz1_ref, dos, lse, delta, vgrads, gup_bias,
        u_ref, dpb_ref, h1b_ref, dmb_ref, dzb_ref, ob_ref,
        wup, wdown, wout, pre_s, prod, sem_up, sem_down, sem_out,
    ) = rest
    width = wup.shape[1] // 2
    owidth = wout.shape[1] // 2
    out_part = [d.at[..., width : width + owidth] for d in downs]
    down_part = [d.at[..., 0:width] for d in downs]
    c_out = piece_copies(ids, out_part, lay_out, wout, sem_out, ctx, rows, owidth)
    c_up = piece_copies(ids, ups, lay_up, wup, sem_up, ctx, rows, width)
    c_down = piece_copies(ids, down_part, lay_down, wdown, sem_down, ctx, rows, width)
    for copy in c_out + c_up + c_down:
        copy.start()
    tokens, model = xt.shape
    pairs = heads // 2
    half = tokens
    parts = []
    for p in range(pairs):
        mass = sums[p, LANES : LANES + 1, :]
        ot = sums[p, 0:LANES, :] / mass
        lse[p] = top[p] + jnp.log(mass)
        parts.append(jnp.concatenate([ot[0:HD, 0:half], ot[HD:LANES, half : 2 * half]], 0).T)
    o = jnp.concatenate(parts, 1)
    ob = o.astype(BF)
    ob_ref[...] = ob
    for copy in c_out:
        copy.wait()
    b_out, g1, b1, b_down, g2, b2 = (vec[i : i + 1, :] for i in range(6))
    z1 = xt[...].astype(F32) + mm(ob, wout[...], NT) + b_out
    n1, f1 = normed(z1)
    h1 = n1 * g1 + b1
    h1b = h1.astype(BF)
    h1b_ref[...] = h1b
    for copy in c_up:
        copy.wait()
    hidden = wup.shape[1]
    step = model
    for c in range(0, hidden, step):
        pre = mm(h1b, wup[:, c : c + step]) + b_up[:, c : c + step]
        pre_s[:, c : c + step] = pre
        u_ref[:, c : c + step] = (0.5 * pre * (1.0 + lax.erf(pre * 0.7071067811865476))).astype(BF)
    for copy in c_down:
        copy.wait()
    m = mm(u_ref[...], wdown[...], NT) + b_down
    n2, f2 = normed(h1 + m)
    out_ref[...] = (n2 * g2 + b2).astype(BF)
    g = cot[...].astype(F32)
    dz2 = norm_back(g, n2, f2, g2)
    dmb = dz2.astype(BF)
    dmb_ref[...] = dmb
    vgrads[3:4, :] = total(dz2)
    vgrads[4:5, :] = total(g * n2)
    vgrads[5:6, :] = total(g)
    for c in range(0, hidden, step):
        pre = pre_s[:, c : c + step]
        slope = 0.5 * (1.0 + lax.erf(pre * 0.7071067811865476)) + pre * jnp.exp(
            -0.5 * pre * pre
        ) * 0.3989422804014327
        dpre = mm(dmb, wdown[:, c : c + step]) * slope
        gup_bias[:, c : c + step] = total(dpre)
        dpb_ref[:, c : c + step] = dpre.astype(BF)
    dh1 = dz2 + mm(dpb_ref[...], wup[...], NT)
    dz1 = norm_back(dh1, n1, f1, g1)
    dz1_ref[...] = dz1
    vgrads[0:1, :] = total(dz1)
    vgrads[1:2, :] = total(dh1 * n1)
    vgrads[2:3, :] = total(dh1)
    vgrads[6:8, :] = jnp.zeros((2, model), F32)
    dzb = dz1.astype(BF)
    dzb_ref[...] = dzb
    do = mm(dzb, wout[...]).astype(BF).astype(F32)
    prod[...] = do * o
    spread = (
        lax.broadcasted_iota(jnp.int32, (16, model), 1) // HD
        == lax.broadcasted_iota(jnp.int32, (16, model), 0)
    ).astype(F32)
    by_head = lax.dot_general(
        spread, prod[...], NT, precision=lax.Precision.HIGHEST, preferred_element_type=F32
    )
    lane = lax.broadcasted_iota(jnp.int32, (tokens, LANES), 1)
    for p in range(pairs):
        two = do[:, p * LANES : (p + 1) * LANES]
        dos[p] = jnp.concatenate(
            [jnp.where(lane < HD, two, 0.0).astype(BF), jnp.where(lane >= HD, two, 0.0).astype(BF)], 0
        )
        delta[p] = jnp.concatenate([by_head[2 * p : 2 * p + 1], by_head[2 * p + 1 : 2 * p + 2]], 1)


def feed_grads_kernel(ctx, rows, lay_up, lay_down, lay_out, ids, h1b, dmb, dzb, ob, u, dpb,
                      up0, up1, down0, down1, gup, gdown, gout, h1t, dmt, sem_up, sem_down, sem_out):
    step = pl.program_id(0)
    model = gup.shape[0]
    width, owidth = gup.shape[1] // 2, gout.shape[1] // 2

    @pl.when(step == 0)
    def _():
        h1t[...] = h1b[...].T
        dmt[...] = dmb[...].T
        gout[...] = mm(dzb[...].T, ob[...]).astype(BF)

    span = pl.ds(pl.multiple_of(step * model, LANES), model)
    gup[:, span] = mm(h1t[...], dpb[...]).astype(BF)
    gdown[:, span] = mm(dmt[...], u[...]).astype(BF)

    @pl.when(step == pl.num_programs(0) - 1)
    def _():
        downs = [down0, down1]
        copies = piece_copies(ids, [up0, up1], lay_up, gup, sem_up, ctx, rows, width, True)
        copies += piece_copies(
            ids, [d.at[..., 0:width] for d in downs], lay_down, gdown, sem_down, ctx, rows, width, True)
        copies += piece_copies(
            ids, [d.at[..., width : width + owidth] for d in downs], lay_out, gout, sem_out, ctx, rows, owidth, True)
        for copy in copies:
            copy.start()
        for copy in copies:
            copy.wait()


def attend_back_kernel(first, keys, values, keys_t, queries, qmark, kmark, dos, lse, delta, wk, wv, *rest):
    if first:
        dk_ref, dv_ref, dqt_out, gbv, dxa, dxb, dx = rest
    else:
        dqt_in, dk_ref, dv_ref, dqt_out, gbv, dxa, dxb, dx = rest
    step = pl.program_id(0)
    k4, v4 = keys[...], values[...]
    dks, dvs = [], []
    for j in range(2):
        span = slice(j * LANES, (j + 1) * LANES)
        kk = jnp.concatenate([k4[:, span], kmark[...]], 1)
        qq = jnp.concatenate([queries[j], qmark[...]], 1)
        probs = jnp.exp(mm(kk, qq, NT) - lse[j])
        ds = (probs * (mm(v4[:, span], dos[j], NT) - delta[j])).astype(BF)
        dvs.append(mm(probs.astype(BF), dos[j]))
        dks.append(mm(ds, queries[j]))
        dqt = mm(keys_t[span], ds)
        dqt_out[j] = dqt if first else dqt_in[j] + dqt
    dv4 = jnp.concatenate(dvs, 1)
    gbv[...] = total(dv4)
    dkb, dvb = jnp.concatenate(dks, 1).astype(BF), dv4.astype(BF)
    dk_ref[...] = dkb
    dv_ref[...] = dvb
    part = mm(dkb, wk[...], NT) + mm(dvb, wv[...], NT)

    @pl.when(step == 0)
    def _():
        dx[...] = part

    @pl.when(step > 0)
    def _():
        dx[...] += part

    @pl.when(step == pl.num_programs(0) - 1)
    def _():
        half = dxa.shape[0]
        dxa[...] = dx[0:half].astype(BF)
        dxb[...] = dx[half:].astype(BF)


def last_kernel(ctx, rows, layout, scale, ids, dqt, wq, *rest):
    blocks = 2 * ctx
    xs, rest = rest[:blocks], rest[blocks:]
    dks, rest = rest[:ctx], rest[ctx:]
    dvs, rest = rest[:ctx], rest[ctx:]
    dxq, gbq, out0, out1, grads, xts, dx, sem = rest
    step = pl.program_id(0)
    half = xs[0].shape[0]

    @pl.when(step == 0)
    def _():
        for i in range(blocks):
            xts[i] = xs[i][...].T

    cols = []
    for j in range(2):
        t = dqt[j]
        cols.append(jnp.concatenate([t[0:HD, 0:half], t[HD:LANES, half : 2 * half]], 0).T)
    dq = jnp.concatenate(cols, 1) * scale
    gbq[...] = total(dq)
    dqb = dq.astype(BF)
    width = dqb.shape[1]
    span = pl.ds(pl.multiple_of(step * width, LANES), width)
    part = mm(dqb, wq[...], NT)

    @pl.when(step == 0)
    def _():
        dx[...] = part

    @pl.when(step > 0)
    def _():
        dx[...] += part

    grads[0, :, span] = mm(xts[0], dqb).astype(BF)
    for kind, parts in ((1, dks), (2, dvs)):
        acc = None
        for r in range(ctx):
            for side in range(2):
                one = mm(xts[2 * r + side], parts[r][side * half : (side + 1) * half, :])
                acc = one if acc is None else acc + one
        grads[kind, :, span] = acc.astype(BF)

    @pl.when(step == pl.num_programs(0) - 1)
    def _():
        dxq[...] = dx[...]
        copies = piece_copies(ids, [out0, out1], layout, grads, sem, ctx, rows, grads.shape[2] // 2, True)
        for copy in copies:
            copy.start()
        for copy in copies:
            copy.wait()


def shift(v, by, ctx):
    return lax.ppermute(v, "ctx", [(i, (i + by) % ctx) for i in range(ctx)])


def swap(v, axis):
    return lax.ppermute(v, axis, SWAP)


def gather_pieces(local, ctx, order, axis):
    rows = local.shape[axis]
    line = jnp.concatenate([local] + [shift(local, r, ctx) for r in range(1, ctx)], axis)
    both = jnp.concatenate([line, swap(line, order[0])], axis)
    far = swap(both, order[1])
    arrays, layout = [], []
    for rc in range(2):
        for second, v in ((0, both), (1, far)):
            arrays.append(v if rc == 0 else swap(v, "core"))
            pieces = []
            for first in range(2):
                for rz in range(ctx):
                    at = (first * ctx + rz) * rows
                    index = (slice(None),) * axis + (slice(at, at + rows),)
                    rel = {order[0]: first, order[1]: second}
                    pieces.append((index, (rc, rel["y"], rel["tensor"], rz)))
            layout.append(pieces)
    return arrays, layout


def scatter_layout(ctx, rows, order, lead):
    layout = []
    for rc in range(2):
        pieces = []
        for first in range(2):
            for second in range(2):
                for rz in range(ctx):
                    rel = {order[0]: first, order[1]: second}
                    index = (first, second) + (slice(None),) * lead + (slice(rz * rows, (rz + 1) * rows),)
                    pieces.append((index, (rc, rel["y"], rel["tensor"], rz)))
        layout.append(pieces)
    return layout


def add(a, b):
    return a.astype(F32) + b.astype(F32)


def scatter_sum(kept, sent, ctx, rows, order, axis):
    summed = add(kept, swap(sent, "core"))
    summed = add(summed[0], swap(summed[1].astype(BF), order[0]))
    summed = add(summed[0], swap(summed[1].astype(BF), order[1]))
    pick = lambda r: lax.slice_in_dim(summed, r * rows, (r + 1) * rows, axis=axis)
    result = pick(0)
    for r in range(1, ctx):
        result = result + shift(pick(r).astype(BF), -r, ctx).astype(F32)
    return result


def sum_everywhere(v, ctx):
    for axis in ("core", "tensor", "y"):
        v = v + swap(v, axis)
    bit = 1
    while bit < ctx:
        v = v + lax.ppermute(v, "ctx", [(i, i ^ bit) for i in range(ctx)])
        bit *= 2
    return v


def on_device(
    layer_input, segments, w_qkv, b_qv, w_out, b_out, ln1_gain, ln1_bias,
    w_up, b_up, w_down, b_down, ln2_gain, ln2_bias, cotangent,
):
    ctx = lax.axis_size("ctx")
    y, core, z, t = (lax.axis_index(a) for a in EVERY)
    ids = jnp.stack([y, core, z, t]).astype(jnp.int32)
    x = layer_input[0]
    tokens = x.shape[0] // 2
    model = x.shape[1]
    heads = model // HD
    pairs = heads // 2
    quads = heads // 4
    quad = 4 * HD
    rows, width, owidth = w_up.shape[0], w_up.shape[1], w_out.shape[1]
    hidden = 2 * width
    length = 2 * tokens
    scale = 1.0 / math.sqrt(HD)

    own = lambda v: lax.dynamic_slice_in_dim(v, t * tokens, tokens)
    other = lambda v: lax.dynamic_slice_in_dim(v, (1 - t) * tokens, tokens)
    xt = own(x)

    wq_arrays, wq_layout = gather_pieces(w_qkv.transpose(1, 0, 2), ctx, ("tensor", "y"), 1)
    ring = [xt]
    for _ in range(1, ctx):
        ring.append(shift(ring[-1], 1, ctx))
    sides = [other(x)] + [swap(v, "tensor") for v in ring[1:]]
    up_arrays, up_layout = gather_pieces(w_up, ctx, ("y", "tensor"), 0)
    down_arrays, down_layout = gather_pieces(
        jnp.concatenate([w_down, w_out], 1), ctx, ("tensor", "y"), 0
    )

    seg = segments[0].reshape(ctx, 2, tokens)[::-1]
    seg = lax.dynamic_slice_in_dim(jnp.concatenate([seg, seg]), ctx - 1 - z, ctx)
    seg = jnp.where(t == 0, seg, seg[:, ::-1])
    mark = jnp.arange(LANES, dtype=jnp.int32)
    kmark = jnp.where(
        (mark < 3) & (seg.reshape(ctx, length)[..., None] != mark), -1e30, 0.0
    ).astype(BF)
    qmark = (seg[0, 0][:, None] == mark).astype(BF)
    qmark = jnp.concatenate([qmark, qmark])

    biases = b_qv.astype(F32)
    biases_other = swap(biases, "tensor")
    biases = jnp.where(
        t == 0,
        jnp.concatenate([biases, biases_other], 1),
        jnp.concatenate([biases_other, biases], 1),
    )
    bup_mine = b_up.astype(F32)[None]
    bup_other = swap(bup_mine, "tensor")
    bup_full = jnp.where(
        t == 0,
        jnp.concatenate([bup_mine, bup_other], 1),
        jnp.concatenate([bup_other, bup_mine], 1),
    )

    n_pieces = 4 * ctx * 2
    weights, queries = pl.pallas_call(
        lambda *refs: prepare_kernel(ctx, rows, owidth, wq_layout, 4, heads, scale, *refs),
        out_shape=(
            jax.ShapeDtypeStruct((3, model, model), BF),
            jax.ShapeDtypeStruct((pairs, length, LANES), BF),
        ),
        in_specs=[scalars(), whole((tokens, model)), whole((1, model))] + [anywhere()] * 4,
        out_specs=(whole((3, model, model)), whole((pairs, length, LANES))),
        scratch_shapes=[pltpu.SemaphoreType.DMA((n_pieces,))],
        compiler_params=params(32),
        name="prepare",
    )(ids, xt, biases[0:1], *wq_arrays)

    def of_kind(kind):
        return pl.BlockSpec((None, model, quad), lambda g: (kind, 0, g))

    columns = pl.BlockSpec((length, quad), lambda g: (0, g))
    rows_t = pl.BlockSpec((quad, length), lambda g: (g, 0))
    row = pl.BlockSpec((1, quad), lambda g: (0, g))
    by_pair = lambda *tail: pl.BlockSpec((2,) + tail, lambda g: (g,) + (0,) * len(tail))

    kv = []
    carry = ()
    state_shapes = (
        jax.ShapeDtypeStruct((pairs, 1, length), F32),
        jax.ShapeDtypeStruct((pairs, LANES + 16, length), F32),
    )
    state_specs = (by_pair(1, length), by_pair(LANES + 16, length))
    for r in range(ctx):
        first = r == 0
        k_r, v_r, kt_r, *carry = pl.pallas_call(
            lambda *refs, first=first: attend_kernel(first, *refs),
            grid=(quads,),
            out_shape=(
                jax.ShapeDtypeStruct((length, model), BF),
                jax.ShapeDtypeStruct((length, model), BF),
                jax.ShapeDtypeStruct((model, length), BF),
            ) + state_shapes,
            in_specs=[
                whole((tokens, model)), whole((tokens, model)), of_kind(1), of_kind(2), row,
                by_pair(length, LANES), whole((length, LANES)), whole((length, LANES)),
            ] + ([] if first else list(state_specs)),
            out_specs=(columns, columns, rows_t) + state_specs,
            compiler_params=params(40),
            name="attend",
        )(ring[r], sides[r], weights, weights, biases[1:2], queries, qmark, kmark[r], *carry)
        kv.append((k_r, v_r, kt_r))
    top, sums = carry

    vec = jnp.stack(
        [b_out, ln1_gain, ln1_bias, b_down, ln2_gain, ln2_bias, ln2_bias, ln2_bias]
    ).astype(F32)
    sds = jax.ShapeDtypeStruct
    mid_shapes = (
        sds((tokens, model), BF), sds((tokens, model), F32), sds((pairs, length, LANES), BF),
        sds((pairs, 1, length), F32), sds((pairs, 1, length), F32), sds((8, model), F32),
        sds((1, hidden), F32), sds((tokens, hidden), BF), sds((tokens, hidden), BF),
        sds((tokens, model), BF), sds((tokens, model), BF), sds((tokens, model), BF),
        sds((tokens, model), BF),
    )
    (out_own, dz1, dos, lse, delta, vgrads, gup_bias, u, dpb, h1b, dmb, dzb, ob) = pl.pallas_call(
        lambda *refs: middle_kernel(ctx, rows, up_layout, down_layout, down_layout, 4, 4, heads, *refs),
        out_shape=mid_shapes,
        in_specs=[
            scalars(), whole(sums.shape), whole(top.shape), whole((tokens, model)),
            whole((tokens, model)), whole((8, model)), whole((1, hidden)),
        ] + [anywhere()] * 8,
        out_specs=tuple(whole(s.shape) for s in mid_shapes),
        scratch_shapes=[
            pltpu.VMEM((model, hidden), BF), pltpu.VMEM((model, hidden), BF),
            pltpu.VMEM((model, model), BF), pltpu.VMEM((tokens, hidden), F32),
            pltpu.VMEM((tokens, model), F32),
            pltpu.SemaphoreType.DMA((n_pieces,)), pltpu.SemaphoreType.DMA((n_pieces,)),
            pltpu.SemaphoreType.DMA((n_pieces,)),
        ],
        compiler_params=params(56),
        name="middle",
    )(ids, sums, top, xt, own(cotangent[0]), vec, bup_full, *up_arrays, *down_arrays)

    up_order, down_order, qkv_order = ("y", "tensor"), ("tensor", "y"), ("y", "tensor")
    lay_up = scatter_layout(ctx, rows, up_order, 0)
    lay_down = scatter_layout(ctx, rows, down_order, 0)
    piece = lambda w: sds((2, 2, ctx * rows, w), BF)
    chunk = pl.BlockSpec((tokens, model), lambda c: (0, c))
    up0, up1, down0, down1 = pl.pallas_call(
        lambda *refs: feed_grads_kernel(ctx, rows, lay_up, lay_down, lay_down, *refs),
        grid=(hidden // model,),
        out_shape=(piece(width), piece(width), piece(width + owidth), piece(width + owidth)),
        in_specs=[scalars()] + [whole((tokens, model))] * 4 + [chunk, chunk],
        out_specs=(anywhere(),) * 4,
        scratch_shapes=[
            pltpu.VMEM((model, hidden), BF), pltpu.VMEM((model, hidden), BF),
            pltpu.VMEM((model, model), BF), pltpu.VMEM((model, tokens), BF),
            pltpu.VMEM((model, tokens), BF),
            pltpu.SemaphoreType.DMA((n_pieces,)), pltpu.SemaphoreType.DMA((n_pieces,)),
            pltpu.SemaphoreType.DMA((n_pieces,)),
        ],
        compiler_params=params(40),
        name="feed_grads",
    )(ids, h1b, dmb, dzb, ob, u, dpb)
    grad_up = scatter_sum(up0, up1, ctx, rows, up_order, 0)
    grad_down = scatter_sum(down0, down1, ctx, rows, down_order, 0)

    dkv, gbv, arrived = [None] * ctx, None, []
    dqt = ()
    own_part = None
    for i, r in enumerate(list(range(1, ctx)) + [0]):
        first = i == 0
        k_r, v_r, kt_r = kv[r]
        dk_r, dv_r, acc, gbv_r, dxa, dxb = pl.pallas_call(
            lambda *refs, first=first: attend_back_kernel(first, *refs),
            grid=(quads,),
            out_shape=(
                sds((length, model), BF), sds((length, model), BF), sds((pairs, LANES, length), F32),
                sds((1, model), F32), sds((tokens, model), BF), sds((tokens, model), BF),
            ),
            in_specs=[
                columns, columns, rows_t, by_pair(length, LANES), whole((length, LANES)),
                whole((length, LANES)), by_pair(length, LANES), by_pair(1, length), by_pair(1, length),
                of_kind(1), of_kind(2),
            ] + ([] if first else [by_pair(LANES, length)]),
            out_specs=(
                columns, columns, by_pair(LANES, length), row, whole((tokens, model)), whole((tokens, model)),
            ),
            scratch_shapes=[pltpu.VMEM((length, model), F32)],
            compiler_params=params(40),
            name="attend_back",
        )(k_r, v_r, kt_r, queries, qmark, kmark[r], dos, lse, delta, weights, weights, *dqt)
        dqt = (acc,)
        dkv[r] = (dk_r, dv_r)
        gbv = gbv_r if gbv is None else gbv + gbv_r
        part = add(dxa, swap(dxb, "tensor"))
        if r == 0:
            own_part = part
        else:
            arrived.append(shift(part.astype(BF), -r, ctx))

    lay_qkv = scatter_layout(ctx, rows, qkv_order, 1)
    piece = sds((2, 2, 3, ctx * rows, owidth), BF)
    dxq, gbq, qkv0, qkv1 = pl.pallas_call(
        lambda *refs: last_kernel(ctx, rows, lay_qkv, scale, *refs),
        grid=(quads,),
        out_shape=(sds((tokens, model), F32), sds((1, model), F32), piece, piece),
        in_specs=[scalars(), by_pair(LANES, length), of_kind(0)]
        + [whole((tokens, model))] * (2 * ctx) + [columns] * (2 * ctx),
        out_specs=(whole((tokens, model)), row, anywhere(), anywhere()),
        scratch_shapes=[
            pltpu.VMEM((3, model, model), BF), pltpu.VMEM((2 * ctx, model, tokens), BF),
            pltpu.VMEM((tokens, model), F32), pltpu.SemaphoreType.DMA((n_pieces,)),
        ],
        compiler_params=params(48),
        name="last",
    )(ids, dqt[0], weights, *[v for pair in zip(ring, sides) for v in pair],
      *[d[0] for d in dkv], *[d[1] for d in dkv])

    grad_in = dz1 + dxq + own_part
    for v in arrived:
        grad_in = grad_in + v.astype(F32)
    grad_qkv = scatter_sum(qkv0, qkv1, ctx, rows, qkv_order, 1).transpose(1, 0, 2)

    vectors = jnp.concatenate([gbq[0], gbv[0], vgrads.reshape(-1), gup_bias[0]])
    vectors = sum_everywhere(vectors.reshape(-1, LANES), ctx).reshape(-1)
    pick = lambda i: vectors[i * model : (i + 1) * model]
    part_of = lambda v, w: lax.dynamic_slice_in_dim(v, t * w, w)
    grad_bqv = jnp.stack([part_of(pick(0), owidth), part_of(pick(1), owidth)])

    def both_halves(mine):
        theirs = swap(mine, "tensor")
        return jnp.where(
            t == 0, jnp.concatenate([mine, theirs]), jnp.concatenate([theirs, mine])
        )[None]

    return (
        both_halves(out_own),
        both_halves(grad_in.astype(BF)).astype(F32),
        grad_qkv,
        grad_bqv,
        grad_down[:, width:],
        pick(2),
        pick(3),
        pick(4),
        grad_up,
        part_of(vectors[10 * model :], width),
        grad_down[:, :width],
        pick(5),
        pick(6),
        pick(7),
    )


neg_large = -1e30


def general_norm(summed, gain, bias):
    centred = summed - jnp.mean(summed, -1, keepdims=True)
    scaling = lax.rsqrt(jnp.mean(centred * centred, -1, keepdims=True) + 1e-05)
    normal_part = centred * scaling
    return (normal_part * gain + bias, normal_part, scaling)


def general_back(upstream, normal_part, scaling, gain):
    scaled = upstream * gain
    inner = (
        scaled
        - jnp.mean(scaled, -1, keepdims=True)
        - normal_part * jnp.mean(scaled * normal_part, -1, keepdims=True)
    )
    return (inner * scaling, jnp.sum(upstream * normal_part, 0), jnp.sum(upstream, 0))


def gelu_exact(inputs):
    return 0.5 * inputs * (1.0 + lax.erf(inputs * 0.7071067811865476))


def gelu_slope(inputs):
    return (
        0.5 * (1.0 + lax.erf(inputs * 0.7071067811865476))
        + inputs * jnp.exp(-0.5 * inputs * inputs) * 0.3989422804014327
    )


def general(
    layer_input,
    segments,
    w_qkv,
    b_qv,
    w_out,
    b_out,
    ln1_gain,
    ln1_bias,
    w_up,
    b_up,
    w_down,
    b_down,
    ln2_gain,
    ln2_bias,
    cotangent,
):
    inputs = layer_input[0]
    tokens = inputs.shape[0]
    group_len = tokens * lax.axis_size("ctx")
    seg_all = segments[0]
    seg_query = lax.dynamic_slice_in_dim(seg_all, lax.axis_index("ctx") * tokens, tokens)
    qkv_full, out_full, up_full, down_full = (
        lax.all_gather(w_qkv, ("shard", "ctx"), axis=0, tiled=True),
        lax.all_gather(w_out, ("shard", "ctx"), axis=0, tiled=True),
        lax.all_gather(w_up, ("shard", "ctx"), axis=0, tiled=True),
        lax.all_gather(w_down, ("shard", "ctx"), axis=0, tiled=True),
    )
    local_width = qkv_full.shape[2]
    heads_here = local_width // HD
    projected = jnp.einsum("td,dwe->wte", inputs, qkv_full, preferred_element_type=jnp.float32)
    bias_pair = b_qv.astype(jnp.float32)
    queries = (projected[0] + bias_pair[0]).astype(jnp.bfloat16)
    key_rows = projected[1].astype(jnp.bfloat16)
    value_rows = (projected[2] + bias_pair[1]).astype(jnp.bfloat16)
    keys_all, values_all = (
        lax.all_gather(key_rows, "ctx", axis=0, tiled=True),
        lax.all_gather(value_rows, "ctx", axis=0, tiled=True),
    )
    query_heads = queries.reshape(tokens, heads_here, HD).transpose(1, 0, 2)
    width_block = min(512, group_len)
    count_blocks = group_len // width_block
    key_blocks = keys_all.reshape(count_blocks, width_block, heads_here, HD)
    value_blocks = values_all.reshape(count_blocks, width_block, heads_here, HD)
    seg_blocks = seg_all.reshape(count_blocks, width_block)

    def scores_of(key_block, seg_block):
        raw = 0.125 * jnp.einsum(
            "htd,khd->htk", query_heads, key_block, preferred_element_type=jnp.float32
        )
        return jnp.where((seg_query[:, None] == seg_block[None, :])[None], raw, neg_large)

    def running_stats(carry, element):
        top_now, mass = carry
        scores = scores_of(element[0], element[1])
        top_next = jnp.maximum(top_now, jnp.max(scores, -1))
        mass = mass * jnp.exp(top_now - top_next) + jnp.sum(
            jnp.exp(scores - top_next[..., None]), -1
        )
        return ((top_next, mass), None)

    start_top = jnp.full((heads_here, tokens), neg_large, jnp.float32)
    (top_final, mass_final), unused = lax.scan(
        running_stats, (start_top, jnp.zeros_like(start_top)), (key_blocks, seg_blocks)
    )
    log_mass = top_final + jnp.log(mass_final)

    def mix_values(accum, element):
        probs = jnp.exp(scores_of(element[0], element[2]) - log_mass[..., None]).astype(
            jnp.bfloat16
        )
        return (
            accum
            + jnp.einsum("htk,khd->htd", probs, element[1], preferred_element_type=jnp.float32),
            None,
        )

    blocks_all = (key_blocks, value_blocks, seg_blocks)
    attended, unused = lax.scan(
        mix_values, jnp.zeros((heads_here, tokens, HD), jnp.float32), blocks_all
    )
    attended_rows = attended.transpose(1, 0, 2).reshape(tokens, local_width).astype(jnp.bfloat16)
    branch_part = jnp.einsum(
        "te,de->td", attended_rows, out_full, preferred_element_type=jnp.float32
    )
    branch = lax.psum(branch_part.astype(jnp.bfloat16), "tensor").astype(
        jnp.float32
    ) + b_out.astype(jnp.float32)
    first_gain = ln1_gain.astype(jnp.float32)
    second_gain = ln2_gain.astype(jnp.float32)
    hidden, first_normal, first_scale = general_norm(
        inputs.astype(jnp.float32) + branch, first_gain, ln1_bias.astype(jnp.float32)
    )
    hidden_low = hidden.astype(jnp.bfloat16)
    pre_act = jnp.dot(hidden_low, up_full, preferred_element_type=jnp.float32) + b_up.astype(
        jnp.float32
    )
    activated = gelu_exact(pre_act).astype(jnp.bfloat16)
    second_part = jnp.einsum("tf,df->td", activated, down_full, preferred_element_type=jnp.float32)
    second_branch = lax.psum(second_part.astype(jnp.bfloat16), "tensor").astype(
        jnp.float32
    ) + b_down.astype(jnp.float32)
    result, second_normal, second_scale = general_norm(
        hidden + second_branch, second_gain, ln2_bias.astype(jnp.float32)
    )
    qkv_full, out_full, up_full, down_full = (
        lax.all_gather(w_qkv, ("shard", "ctx"), axis=0, tiled=True),
        lax.all_gather(w_out, ("shard", "ctx"), axis=0, tiled=True),
        lax.all_gather(w_up, ("shard", "ctx"), axis=0, tiled=True),
        lax.all_gather(w_down, ("shard", "ctx"), axis=0, tiled=True),
    )
    upstream = cotangent[0].astype(jnp.float32)
    second_grad, grad_gain_two, grad_bias_two = general_back(
        upstream, second_normal, second_scale, second_gain
    )
    grad_down_bias = jnp.sum(second_grad, 0)
    second_low = second_grad.astype(jnp.bfloat16)
    grad_down = jnp.einsum("td,tf->df", second_low, activated, preferred_element_type=jnp.float32)
    act_grad = jnp.einsum("td,df->tf", second_low, down_full, preferred_element_type=jnp.float32)
    pre_grad = act_grad * gelu_slope(pre_act)
    grad_up_bias = jnp.sum(pre_grad, 0)
    pre_low = pre_grad.astype(jnp.bfloat16)
    grad_up = jnp.einsum("td,tf->df", hidden_low, pre_low, preferred_element_type=jnp.float32)
    hidden_part = jnp.einsum("tf,df->td", pre_low, up_full, preferred_element_type=jnp.float32)
    hidden_grad = second_grad + lax.psum(hidden_part.astype(jnp.bfloat16), "tensor").astype(
        jnp.float32
    )
    first_grad, grad_gain_one, grad_bias_one = general_back(
        hidden_grad, first_normal, first_scale, first_gain
    )
    grad_out_bias = jnp.sum(first_grad, 0)
    first_low = first_grad.astype(jnp.bfloat16)
    grad_out = jnp.einsum("td,te->de", first_low, attended_rows, preferred_element_type=jnp.float32)
    attended_grad = jnp.einsum(
        "td,de->te", first_low, out_full, preferred_element_type=jnp.float32
    ).astype(jnp.bfloat16)
    grad_heads = attended_grad.reshape(tokens, heads_here, HD).transpose(1, 0, 2)
    row_delta = jnp.sum(grad_heads.astype(jnp.float32) * attended, -1)

    def prob_pair(element):
        probs = jnp.exp(scores_of(element[0], element[2]) - log_mass[..., None])
        prob_grad = jnp.einsum(
            "htd,khd->htk", grad_heads, element[1], preferred_element_type=jnp.float32
        )
        return (probs, prob_grad)

    zero_heads = jnp.zeros((heads_here, tokens, HD), jnp.float32)

    def score_grads(accum, element):
        probs, prob_grad = prob_pair(element)
        score_grad = (probs * (prob_grad - row_delta[..., None])).astype(jnp.bfloat16)
        accum = accum + 0.125 * jnp.einsum(
            "htk,khd->htd", score_grad, element[0], preferred_element_type=jnp.float32
        )
        key_grad = 0.125 * jnp.einsum(
            "htk,htd->khd", score_grad, query_heads, preferred_element_type=jnp.float32
        )
        value_grad = jnp.einsum(
            "htk,htd->khd",
            probs.astype(jnp.bfloat16),
            grad_heads,
            preferred_element_type=jnp.float32,
        )
        return (accum, (key_grad, value_grad))

    query_grad, (key_parts, value_parts) = lax.scan(score_grads, zero_heads, blocks_all)
    key_sum, value_sum = (
        lax.psum_scatter(
            key_parts.reshape(group_len, local_width).astype(jnp.bfloat16),
            "ctx",
            scatter_dimension=0,
            tiled=True,
        ).astype(jnp.float32),
        lax.psum_scatter(
            value_parts.reshape(group_len, local_width).astype(jnp.bfloat16),
            "ctx",
            scatter_dimension=0,
            tiled=True,
        ).astype(jnp.float32),
    )
    query_rows = query_grad.transpose(1, 0, 2).reshape(tokens, local_width)
    bias_grads = jnp.stack([jnp.sum(query_rows, 0), jnp.sum(value_sum, 0)])
    stacked = jnp.stack([query_rows, key_sum, value_sum]).astype(jnp.bfloat16)
    grad_qkv = jnp.einsum("td,wte->dwe", inputs, stacked, preferred_element_type=jnp.float32)
    input_part = jnp.einsum("wte,dwe->td", stacked, qkv_full, preferred_element_type=jnp.float32)
    grad_inputs = first_grad + lax.psum(input_part.astype(jnp.bfloat16), "tensor").astype(
        jnp.float32
    )
    matrices = (
        lax.psum_scatter(grad_qkv, ("shard", "ctx"), scatter_dimension=0, tiled=True),
        lax.psum_scatter(grad_out, ("shard", "ctx"), scatter_dimension=0, tiled=True),
        lax.psum_scatter(grad_up, ("shard", "ctx"), scatter_dimension=0, tiled=True),
        lax.psum_scatter(grad_down, ("shard", "ctx"), scatter_dimension=0, tiled=True),
    )
    vectors = lax.psum(
        (
            bias_grads,
            grad_out_bias,
            grad_gain_one,
            grad_bias_one,
            grad_up_bias,
            grad_down_bias,
            grad_gain_two,
            grad_bias_two,
        ),
        ("shard", "ctx"),
    )
    return (
        result.astype(jnp.bfloat16)[None],
        grad_inputs[None],
        matrices[0],
        vectors[0],
        matrices[1],
        vectors[1],
        vectors[2],
        vectors[3],
        matrices[2],
        vectors[4],
        matrices[3],
        vectors[5],
        vectors[6],
        vectors[7],
    )


def solution(mesh):
    sizes = dict(mesh.shape)
    ctx = sizes["ctx"]
    fits = sizes["shard"] == 4 and sizes["tensor"] == 2 and ctx & (ctx - 1) == 0
    if fits:
        mesh = Mesh(mesh.devices.reshape(2, 2, ctx, 2), EVERY)
        shard, body = ("y", "core"), on_device
        rows = ("y", "core", "ctx")
    else:
        shard, body = "shard", general
        rows = ("shard", "ctx")
    activations, matrix = P(shard, "ctx", None), P(rows, "tensor")
    cube, pair = P(rows, None, "tensor"), P(None, "tensor")
    return jax.shard_map(
        body,
        mesh=mesh,
        in_specs=(
            activations, P(shard, None), cube, pair, matrix, P(), P(), P(), matrix, P("tensor"),
            matrix, P(), P(), P(), activations,
        ),
        out_specs=(
            activations, activations, cube, pair, matrix, P(), P(), P(), matrix, P("tensor"),
            matrix, P(), P(), P(),
        ),
        check_vma=False,
    )
```

```python
import math

import jax
import jax.numpy as jnp
from jax import lax
from jax.experimental import pallas as pl
from jax.experimental.pallas import tpu as pltpu
from jax.sharding import Mesh
from jax.sharding import PartitionSpec as P

HD = 64
LANES = 128
BF = jnp.bfloat16
F32 = jnp.float32
NT = (((1,), (1,)), ((), ()))
NN = (((1,), (0,)), ((), ()))
EVERY = ("y", "core", "ctx", "tensor")
SWAP = ((0, 1), (1, 0))


def mm(a, b, dims=NN):
    return lax.dot_general(a, b, dims, preferred_element_type=F32)


def cost(flops, size):
    return pl.CostEstimate(flops=int(flops * 0.4), bytes_accessed=int(size * 0.4), transcendentals=0)


def params(mib):
    return pltpu.CompilerParams(vmem_limit_bytes=mib << 20)


def anywhere():
    return pl.BlockSpec(memory_space=pl.ANY)


def whole(shape):
    return pl.BlockSpec(shape, lambda *_: (0,) * len(shape))


def scalars():
    return pl.BlockSpec(memory_space=pltpu.SMEM)


def owner_of(ids, piece, ctx):
    rc, ry, rx, rz = piece
    y = (ids[0] + ry) % 2
    core = (ids[1] + rc) % 2
    place = (ids[2] + (ctx - rz)) % ctx
    return (y * 2 + core) * ctx + place, (ids[3] + rx) % 2


def piece_copies(ids, refs, layout, full, sem, ctx, rows, width, back=False, base=0):
    copies = []
    for ref, pieces, at in zip(refs, layout, range(len(refs))):
        for index, piece in pieces:
            block, half = piece if len(piece) == 2 else owner_of(ids, piece, ctx)
            row, column = block * rows, half * width
            if len(piece) > 2:
                row, column = pl.multiple_of(row, 16), pl.multiple_of(column, LANES)
            if len(full.shape) == 3:
                there = full.at[:, pl.ds(row, rows), pl.ds(column, width)]
            else:
                there = full.at[pl.ds(row, rows), pl.ds(column, width)]
            here = ref.at[index]
            source, target = (there, here) if back else (here, there)
            copies.append(pltpu.make_async_copy(source, target, sem.at[base + len(copies)]))
    return copies


def prepare_kernel(ctx, rows, width, layout, n, heads, scale, ids, xt, bq, *rest):
    pieces, (weights, queries, sem) = rest[:n], rest[n:]
    copies = piece_copies(ids, pieces, layout, weights, sem, ctx, rows, width)
    for copy in copies:
        copy.start()
    for copy in copies:
        copy.wait()
    tokens = xt.shape[0]
    lane = lax.broadcasted_iota(jnp.int32, (tokens, LANES), 1)
    projected = mm(xt[...], weights[0]) + bq[...]
    projected = (projected.astype(BF).astype(F32) * scale)
    for pair in range(heads // 2):
        two = projected[:, pair * LANES : (pair + 1) * LANES]
        even = jnp.where(lane < HD, two, 0.0).astype(BF)
        odd = jnp.where(lane >= HD, two, 0.0).astype(BF)
        queries[pair] = jnp.concatenate([even, odd], 0)


def attend_kernel(first, xa, xb, wk, wv, bv, queries, qmark, kmark, *rest):
    if first:
        keys, values, keys_t, top_out, sums_out = rest
    else:
        top_in, sums_in, keys, values, keys_t, top_out, sums_out = rest
    x = jnp.concatenate([xa[...], xb[...]], 0)
    k4 = mm(x, wk[...]).astype(BF)
    v4 = mm(x, wv[...]) + bv[...]
    keys[...] = k4
    values[...] = v4.astype(BF)
    keys_t[...] = k4.T
    v4t = v4.T.astype(BF)
    ones = jnp.ones((16, x.shape[0]), BF)
    for j in range(2):
        span = slice(j * LANES, (j + 1) * LANES)
        kk = jnp.concatenate([k4[:, span], kmark[...]], 1)
        qq = jnp.concatenate([queries[j], qmark[...]], 1)
        scores = mm(kk, qq, NT)
        top = jnp.max(scores, 0, keepdims=True)
        if not first:
            top = jnp.maximum(top, top_in[j])
        probs = jnp.exp(scores - top).astype(BF)
        sums = mm(jnp.concatenate([v4t[span], ones], 0), probs)
        if not first:
            sums = sums + sums_in[j] * jnp.exp(top_in[j] - top)
        top_out[j] = top
        sums_out[j] = sums


def normed(z, eps=1e-05):
    centred = z - jnp.mean(z, -1, keepdims=True)
    factor = lax.rsqrt(jnp.mean(centred * centred, -1, keepdims=True) + eps)
    return centred * factor, factor


def norm_back(e, n, factor, gain):
    scaled = e * gain
    return factor * (
        scaled - jnp.mean(scaled, -1, keepdims=True) - n * jnp.mean(scaled * n, -1, keepdims=True)
    )


def total(v):
    return jnp.sum(v, 0, keepdims=True)


def middle_kernel(ctx, rows, lay_up, lay_down, lay_out, n, heads, ids, sums, top, xt, cot, vec, b_up, *rest):
    feeds, rest = rest[:n], rest[n:]
    (
        out_ref, dz1_ref, dos, lse, delta, vgrads, gup_bias,
        u_ref, dpb_ref, h1b_ref, dmb_ref, dzb_ref, ob_ref,
        wup, wdown, wout, pre_s, prod, sem_up, sem_down, sem_out,
    ) = rest
    width = wup.shape[1] // 2
    owidth = wout.shape[1] // 2
    up_part, out_part, down_part = (
        [d.at[:, a:b] for d in feeds]
        for a, b in ((0, width), (width, width + owidth), (width + owidth, 2 * width + owidth))
    )
    c_out = piece_copies(ids, out_part, lay_out, wout, sem_out, ctx, rows, owidth)
    c_up = piece_copies(ids, up_part, lay_up, wup, sem_up, ctx, rows, width)
    c_down = piece_copies(ids, down_part, lay_down, wdown, sem_down, ctx, rows, width)
    for copy in c_out + c_up + c_down:
        copy.start()
    tokens, model = xt.shape
    pairs = heads // 2
    half = tokens
    parts = []
    for p in range(pairs):
        mass = sums[p, LANES : LANES + 1, :]
        ot = sums[p, 0:LANES, :] / mass
        lse[p] = top[p] + jnp.log(mass)
        parts.append(jnp.concatenate([ot[0:HD, 0:half], ot[HD:LANES, half : 2 * half]], 0).T)
    o = jnp.concatenate(parts, 1)
    ob = o.astype(BF)
    ob_ref[...] = ob
    for copy in c_out:
        copy.wait()
    b_out, g1, b1, b_down, g2, b2 = (vec[i : i + 1, :] for i in range(6))
    z1 = xt[...].astype(F32) + mm(ob, wout[...], NT) + b_out
    n1, f1 = normed(z1)
    h1 = n1 * g1 + b1
    h1b = h1.astype(BF)
    h1b_ref[...] = h1b
    for copy in c_up:
        copy.wait()
    hidden = wup.shape[1]
    step = model
    for c in range(0, hidden, step):
        pre = mm(h1b, wup[:, c : c + step]) + b_up[:, c : c + step]
        pre_s[:, c : c + step] = pre
        u_ref[:, c : c + step] = (0.5 * pre * (1.0 + lax.erf(pre * 0.7071067811865476))).astype(BF)
    for copy in c_down:
        copy.wait()
    m = mm(u_ref[...], wdown[...], NT) + b_down
    n2, f2 = normed(h1 + m)
    out_ref[...] = (n2 * g2 + b2).astype(BF)
    g = cot[...].astype(F32)
    dz2 = norm_back(g, n2, f2, g2)
    dmb = dz2.astype(BF)
    dmb_ref[...] = dmb
    vgrads[3:4, :] = total(dz2)
    vgrads[4:5, :] = total(g * n2)
    vgrads[5:6, :] = total(g)
    for c in range(0, hidden, step):
        pre = pre_s[:, c : c + step]
        slope = 0.5 * (1.0 + lax.erf(pre * 0.7071067811865476)) + pre * jnp.exp(
            -0.5 * pre * pre
        ) * 0.3989422804014327
        dpre = mm(dmb, wdown[:, c : c + step]) * slope
        gup_bias[:, c : c + step] = total(dpre)
        dpb_ref[:, c : c + step] = dpre.astype(BF)
    dh1 = dz2 + mm(dpb_ref[...], wup[...], NT)
    dz1 = norm_back(dh1, n1, f1, g1)
    dz1_ref[...] = dz1
    vgrads[0:1, :] = total(dz1)
    vgrads[1:2, :] = total(dh1 * n1)
    vgrads[2:3, :] = total(dh1)
    vgrads[6:8, :] = jnp.zeros((2, model), F32)
    dzb = dz1.astype(BF)
    dzb_ref[...] = dzb
    do = mm(dzb, wout[...]).astype(BF).astype(F32)
    prod[...] = do * o
    spread = (
        lax.broadcasted_iota(jnp.int32, (16, model), 1) // HD
        == lax.broadcasted_iota(jnp.int32, (16, model), 0)
    ).astype(F32)
    by_head = lax.dot_general(
        spread, prod[...], NT, precision=lax.Precision.HIGHEST, preferred_element_type=F32
    )
    lane = lax.broadcasted_iota(jnp.int32, (tokens, LANES), 1)
    for p in range(pairs):
        two = do[:, p * LANES : (p + 1) * LANES]
        dos[p] = jnp.concatenate(
            [jnp.where(lane < HD, two, 0.0).astype(BF), jnp.where(lane >= HD, two, 0.0).astype(BF)], 0
        )
        delta[p] = jnp.concatenate([by_head[2 * p : 2 * p + 1], by_head[2 * p + 1 : 2 * p + 2]], 1)


def feed_grads_kernel(ctx, rows, lay_up, lay_down, lay_out, ids, h1b, dmb, dzb, ob, u, dpb,
                      up0, up1, down0, down1, gup, gdown, gout, h1t, dmt, sem_up, sem_down, sem_out):
    step = pl.program_id(0)
    model = gup.shape[0]
    width, owidth = gup.shape[1] // 2, gout.shape[1] // 2

    @pl.when(step == 0)
    def _():
        h1t[...] = h1b[...].T
        dmt[...] = dmb[...].T
        gout[...] = mm(dzb[...].T, ob[...]).astype(BF)

    span = pl.ds(pl.multiple_of(step * model, LANES), model)
    gup[:, span] = mm(h1t[...], dpb[...]).astype(BF)
    gdown[:, span] = mm(dmt[...], u[...]).astype(BF)

    @pl.when(step == pl.num_programs(0) - 1)
    def _():
        downs = [down0, down1]
        copies = piece_copies(ids, [up0, up1], lay_up, gup, sem_up, ctx, rows, width, True)
        copies += piece_copies(
            ids, [d.at[..., 0:width] for d in downs], lay_down, gdown, sem_down, ctx, rows, width, True)
        copies += piece_copies(
            ids, [d.at[..., width : width + owidth] for d in downs], lay_out, gout, sem_out, ctx, rows, owidth, True)
        for copy in copies:
            copy.start()
        for copy in copies:
            copy.wait()


def attend_back_kernel(first, keys, values, keys_t, queries, qmark, kmark, dos, lse, delta, wk, wv, *rest):
    if first:
        dk_ref, dv_ref, dqt_out, gbv, dxa, dxb, dx = rest
    else:
        dqt_in, dk_ref, dv_ref, dqt_out, gbv, dxa, dxb, dx = rest
    step = pl.program_id(0)
    k4, v4 = keys[...], values[...]
    dks, dvs = [], []
    for j in range(2):
        span = slice(j * LANES, (j + 1) * LANES)
        kk = jnp.concatenate([k4[:, span], kmark[...]], 1)
        qq = jnp.concatenate([queries[j], qmark[...]], 1)
        probs = jnp.exp(mm(kk, qq, NT) - lse[j])
        ds = (probs * (mm(v4[:, span], dos[j], NT) - delta[j])).astype(BF)
        dvs.append(mm(probs.astype(BF), dos[j]))
        dks.append(mm(ds, queries[j]))
        dqt = mm(keys_t[span], ds)
        dqt_out[j] = dqt if first else dqt_in[j] + dqt
    dv4 = jnp.concatenate(dvs, 1)
    gbv[...] = total(dv4)
    dkb, dvb = jnp.concatenate(dks, 1).astype(BF), dv4.astype(BF)
    dk_ref[...] = dkb
    dv_ref[...] = dvb
    part = mm(dkb, wk[...], NT) + mm(dvb, wv[...], NT)

    @pl.when(step == 0)
    def _():
        dx[...] = part

    @pl.when(step > 0)
    def _():
        dx[...] += part

    @pl.when(step == pl.num_programs(0) - 1)
    def _():
        half = dxa.shape[0]
        dxa[...] = dx[0:half].astype(BF)
        dxb[...] = dx[half:].astype(BF)


def last_kernel(ctx, rows, layout, scale, ids, dqt, wq, *rest):
    blocks = 2 * ctx
    xs, rest = rest[:blocks], rest[blocks:]
    dks, rest = rest[:ctx], rest[ctx:]
    dvs, rest = rest[:ctx], rest[ctx:]
    dxq, gbq, out0, out1, grads, xts, dx, sem = rest
    step = pl.program_id(0)
    half = xs[0].shape[0]

    @pl.when(step == 0)
    def _():
        for i in range(blocks):
            xts[i] = xs[i][...].T

    cols = []
    for j in range(2):
        t = dqt[j]
        cols.append(jnp.concatenate([t[0:HD, 0:half], t[HD:LANES, half : 2 * half]], 0).T)
    dq = jnp.concatenate(cols, 1) * scale
    gbq[...] = total(dq)
    dqb = dq.astype(BF)
    width = dqb.shape[1]
    span = pl.ds(pl.multiple_of(step * width, LANES), width)
    part = mm(dqb, wq[...], NT)

    @pl.when(step == 0)
    def _():
        dx[...] = part

    @pl.when(step > 0)
    def _():
        dx[...] += part

    grads[0, :, span] = mm(xts[0], dqb).astype(BF)
    for kind, parts in ((1, dks), (2, dvs)):
        acc = None
        for r in range(ctx):
            for side in range(2):
                one = mm(xts[2 * r + side], parts[r][side * half : (side + 1) * half, :])
                acc = one if acc is None else acc + one
        grads[kind, :, span] = acc.astype(BF)

    @pl.when(step == pl.num_programs(0) - 1)
    def _():
        dxq[...] = dx[...]
        copies = piece_copies(ids, [out0, out1], layout, grads, sem, ctx, rows, grads.shape[2] // 2, True)
        for copy in copies:
            copy.start()
        for copy in copies:
            copy.wait()


def shift(v, by, ctx):
    return lax.ppermute(v, "ctx", [(i, (i + by) % ctx) for i in range(ctx)])


def swap(v, axis):
    return lax.ppermute(v, axis, SWAP)


def after(v, *done):
    return lax.optimization_barrier((v,) + done)[0]


def spread_pieces(line, ctx, rows, order, axis):
    both = jnp.concatenate([line, swap(line, order[0])], axis)
    far = swap(both, order[1])
    arrays, layout = [], []
    for rc in range(2):
        for second, v in ((0, both), (1, far)):
            arrays.append(v if rc == 0 else swap(v, "core"))
            pieces = []
            for first in range(2):
                for rz in range(ctx):
                    at = (first * ctx + rz) * rows
                    index = (slice(None),) * axis + (slice(at, at + rows),)
                    rel = {order[0]: first, order[1]: second}
                    pieces.append((index, (rc, rel["y"], rel["tensor"], rz)))
            layout.append(pieces)
    return arrays, layout


def spread_square(line, ctx, rows, axis):
    over_x, over_y = swap(line, "tensor"), swap(line, "y")
    over_both = swap(over_x, "y")
    arrays, layout = [], []
    for rx, ry, v in ((0, 0, line), (1, 0, over_x), (0, 1, over_y), (1, 1, over_both)):
        for rc in range(2):
            arrays.append(v if rc == 0 else swap(v, "core"))
            layout.append([
                ((slice(None),) * axis + (slice(rz * rows, (rz + 1) * rows),), (rc, ry, rx, rz))
                for rz in range(ctx)
            ])
    return arrays, layout


def scatter_layout(ctx, rows, order, lead):
    layout = []
    for rc in range(2):
        pieces = []
        for first in range(2):
            for second in range(2):
                for rz in range(ctx):
                    rel = {order[0]: first, order[1]: second}
                    index = (first, second) + (slice(None),) * lead + (slice(rz * rows, (rz + 1) * rows),)
                    pieces.append((index, (rc, rel["y"], rel["tensor"], rz)))
        layout.append(pieces)
    return layout


def add(a, b):
    return a.astype(F32) + b.astype(F32)


def send_half(terms, axis):
    sent = terms[0][1].astype(F32)
    for v in terms[1:]:
        sent = sent + v[1].astype(F32)
    return [v[0] for v in terms] + [swap(sent.astype(BF), axis)]


def send_line(terms, ctx, rows, axis):
    cut = lambda v, r: lax.slice_in_dim(v, r * rows, (r + 1) * rows, axis=axis).astype(F32)
    sums = [sum(cut(v, r) for v in terms) for r in range(ctx)]
    result = sums[0]
    for r in range(1, ctx):
        result = result + shift(sums[r].astype(BF), -r, ctx).astype(F32)
    return result


def sum_everywhere(v, ctx):
    for axis in ("core", "tensor", "y"):
        v = v + swap(v, axis)
    bit = 1
    while bit < ctx:
        v = v + lax.ppermute(v, "ctx", [(i, i ^ bit) for i in range(ctx)])
        bit *= 2
    return v


def on_device(
    layer_input, segments, w_qkv, b_qv, w_out, b_out, ln1_gain, ln1_bias,
    w_up, b_up, w_down, b_down, ln2_gain, ln2_bias, cotangent,
):
    ctx = lax.axis_size("ctx")
    y, core, z, t = (lax.axis_index(a) for a in EVERY)
    ids = jnp.stack([y, core, z, t]).astype(jnp.int32)
    x = layer_input[0]
    tokens = x.shape[0] // 2
    model = x.shape[1]
    heads = model // HD
    pairs = heads // 2
    quads = heads // 4
    quad = 4 * HD
    rows, width, owidth = w_up.shape[0], w_up.shape[1], w_out.shape[1]
    hidden = 2 * width
    length = 2 * tokens
    scale = 1.0 / math.sqrt(HD)

    own = lambda v: lax.dynamic_slice_in_dim(v, t * tokens, tokens)
    other = lambda v: lax.dynamic_slice_in_dim(v, (1 - t) * tokens, tokens)
    xt = own(x)

    w_local = w_qkv.transpose(1, 0, 2)
    q_line = jnp.concatenate([w_local] + [shift(w_local, r, ctx) for r in range(1, ctx)], 1)
    wq_arrays, wq_layout = spread_square(q_line, ctx, rows, 1)
    feed = lax.all_gather(jnp.concatenate([w_up, w_out, w_down], 1), EVERY, axis=0, tiled=True)
    feed_layout = [[
        ((slice(k * rows, (k + 1) * rows),), (k // 2, k % 2)) for k in range(8 * ctx)
    ]]
    ring = [xt]
    for _ in range(1, ctx):
        ring.append(shift(ring[-1], 1, ctx))
    sides = [other(x)] + [swap(v, "tensor") for v in ring[1:]]
    seg = segments[0].reshape(ctx, 2, tokens)[::-1]
    seg = lax.dynamic_slice_in_dim(jnp.concatenate([seg, seg]), ctx - 1 - z, ctx)
    seg = jnp.where(t == 0, seg, seg[:, ::-1])
    mark = jnp.arange(LANES, dtype=jnp.int32)
    kmark = jnp.where(
        (mark < 3) & (seg.reshape(ctx, length)[..., None] != mark), -1e30, 0.0
    ).astype(BF)
    qmark = (seg[0, 0][:, None] == mark).astype(BF)
    qmark = jnp.concatenate([qmark, qmark])

    mine = jnp.concatenate([b_qv.reshape(1, -1), b_up.reshape(1, -1)], 1)
    mine = jnp.concatenate([mine, jnp.zeros_like(mine)]).astype(F32)
    theirs = swap(mine, "tensor")
    lower, upper = jnp.where(t == 0, mine, theirs)[:1], jnp.where(t == 0, theirs, mine)[:1]
    cut = lambda a, b: jnp.concatenate([lower[:, a:b], upper[:, a:b]], 1)
    biases = jnp.concatenate([cut(0, owidth), cut(owidth, 2 * owidth)])
    bup_full = cut(2 * owidth, 2 * owidth + width)

    n_pieces = 4 * ctx * 2
    weights, queries = pl.pallas_call(
        lambda *refs: prepare_kernel(ctx, rows, owidth, wq_layout, 8, heads, scale, *refs),
        out_shape=(
            jax.ShapeDtypeStruct((3, model, model), BF),
            jax.ShapeDtypeStruct((pairs, length, LANES), BF),
        ),
        in_specs=[scalars(), whole((tokens, model)), whole((1, model))] + [anywhere()] * 8,
        out_specs=(whole((3, model, model)), whole((pairs, length, LANES))),
        scratch_shapes=[pltpu.SemaphoreType.DMA((n_pieces,))],
        compiler_params=params(60),
        cost_estimate=cost(3e+09, 5e+06),
        name="prepare",
    )(ids, xt, biases[0:1], *wq_arrays)

    def of_kind(kind):
        return pl.BlockSpec((None, model, quad), lambda g: (kind, 0, g))

    columns = pl.BlockSpec((length, quad), lambda g: (0, g))
    rows_t = pl.BlockSpec((quad, length), lambda g: (g, 0))
    row = pl.BlockSpec((1, quad), lambda g: (0, g))
    by_pair = lambda *tail: pl.BlockSpec((2,) + tail, lambda g: (g,) + (0,) * len(tail))

    kv = []
    carry = ()
    state_shapes = (
        jax.ShapeDtypeStruct((pairs, 1, length), F32),
        jax.ShapeDtypeStruct((pairs, LANES + 16, length), F32),
    )
    state_specs = (by_pair(1, length), by_pair(LANES + 16, length))
    for r in range(ctx):
        first = r == 0
        k_r, v_r, kt_r, *carry = pl.pallas_call(
            lambda *refs, first=first: attend_kernel(first, *refs),
            grid=(quads,),
            out_shape=(
                jax.ShapeDtypeStruct((length, model), BF),
                jax.ShapeDtypeStruct((length, model), BF),
                jax.ShapeDtypeStruct((model, length), BF),
            ) + state_shapes,
            in_specs=[
                whole((tokens, model)), whole((tokens, model)), of_kind(1), of_kind(2), row,
                by_pair(length, LANES), whole((length, LANES)), whole((length, LANES)),
            ] + ([] if first else list(state_specs)),
            out_specs=(columns, columns, rows_t) + state_specs,
            compiler_params=params(60),
            cost_estimate=cost(5.5e+09, 4e+06),
        name="attend",
        )(ring[r], sides[r], weights, weights, biases[1:2], queries, qmark, kmark[r], *carry)
        kv.append((k_r, v_r, kt_r))
    top, sums = carry

    vec = jnp.stack(
        [b_out, ln1_gain, ln1_bias, b_down, ln2_gain, ln2_bias, ln2_bias, ln2_bias]
    ).astype(F32)
    sds = jax.ShapeDtypeStruct
    mid_shapes = (
        sds((tokens, model), BF), sds((tokens, model), F32), sds((pairs, length, LANES), BF),
        sds((pairs, 1, length), F32), sds((pairs, 1, length), F32), sds((8, model), F32),
        sds((1, hidden), F32), sds((tokens, hidden), BF), sds((tokens, hidden), BF),
        sds((tokens, model), BF), sds((tokens, model), BF), sds((tokens, model), BF),
        sds((tokens, model), BF),
    )
    (out_own, dz1, dos, lse, delta, vgrads, gup_bias, u, dpb, h1b, dmb, dzb, ob) = pl.pallas_call(
        lambda *refs: middle_kernel(ctx, rows, feed_layout, feed_layout, feed_layout, 1, heads, *refs),
        out_shape=mid_shapes,
        in_specs=[
            scalars(), whole(sums.shape), whole(top.shape), whole((tokens, model)),
            whole((tokens, model)), whole((8, model)), whole((1, hidden)),
        ] + [anywhere()],
        out_specs=tuple(whole(s.shape) for s in mid_shapes),
        scratch_shapes=[
            pltpu.VMEM((model, hidden), BF), pltpu.VMEM((model, hidden), BF),
            pltpu.VMEM((model, model), BF), pltpu.VMEM((tokens, hidden), F32),
            pltpu.VMEM((tokens, model), F32),
            pltpu.SemaphoreType.DMA((n_pieces,)), pltpu.SemaphoreType.DMA((n_pieces,)),
            pltpu.SemaphoreType.DMA((n_pieces,)),
        ],
        compiler_params=params(60),
        cost_estimate=cost(1.6e+10, 1.6e+07),
        name="middle",
    )(ids, sums, top, xt, own(cotangent[0]), vec, bup_full, feed)

    up_order, down_order, qkv_order = ("y", "tensor"), ("y", "tensor"), ("y", "tensor")
    lay_up = scatter_layout(ctx, rows, up_order, 0)
    lay_down = scatter_layout(ctx, rows, down_order, 0)
    piece = lambda w: sds((2, 2, ctx * rows, w), BF)
    chunk = pl.BlockSpec((tokens, model), lambda c: (0, c))
    up0, up1, down0, down1 = pl.pallas_call(
        lambda *refs: feed_grads_kernel(ctx, rows, lay_up, lay_down, lay_down, *refs),
        grid=(hidden // model,),
        out_shape=(piece(width), piece(width), piece(width + owidth), piece(width + owidth)),
        in_specs=[scalars()] + [whole((tokens, model))] * 4 + [chunk, chunk],
        out_specs=(anywhere(),) * 4,
        scratch_shapes=[
            pltpu.VMEM((model, hidden), BF), pltpu.VMEM((model, hidden), BF),
            pltpu.VMEM((model, model), BF), pltpu.VMEM((model, tokens), BF),
            pltpu.VMEM((model, tokens), BF),
            pltpu.SemaphoreType.DMA((n_pieces,)), pltpu.SemaphoreType.DMA((n_pieces,)),
            pltpu.SemaphoreType.DMA((n_pieces,)),
        ],
        compiler_params=params(60),
        cost_estimate=cost(9e+09, 1.2e+07),
        name="feed_grads",
    )(ids, h1b, dmb, dzb, ob, u, dpb)
    up_terms = [up0, swap(up1, "core")]
    down_terms = [down0, swap(down1, "core")]

    def both_halves(mine):
        theirs = swap(mine, "tensor")
        return jnp.where(
            t == 0, jnp.concatenate([mine, theirs]), jnp.concatenate([theirs, mine])
        )[None]

    result = both_halves(out_own)

    dkv, gbv, arrived, arrived_x = [None] * ctx, None, [], []
    delta = after(delta, up1)
    dqt = ()
    own_part = None
    for i, r in enumerate(list(range(1, ctx)) + [0]):
        first = i == 0
        if i == 1:
            dos = after(dos, up_terms[-1], down_terms[-1])
            up_terms = send_half(up_terms, up_order[0])
        elif i > 1:
            dos = after(dos, arrived_x[-1], *((result,) if i == 2 else ()))
        k_r, v_r, kt_r = kv[r]
        dk_r, dv_r, acc, gbv_r, dxa, dxb = pl.pallas_call(
            lambda *refs, first=first: attend_back_kernel(first, *refs),
            grid=(quads,),
            out_shape=(
                sds((length, model), BF), sds((length, model), BF), sds((pairs, LANES, length), F32),
                sds((1, model), F32), sds((tokens, model), BF), sds((tokens, model), BF),
            ),
            in_specs=[
                columns, columns, rows_t, by_pair(length, LANES), whole((length, LANES)),
                whole((length, LANES)), by_pair(length, LANES), by_pair(1, length), by_pair(1, length),
                of_kind(1), of_kind(2),
            ] + ([] if first else [by_pair(LANES, length)]),
            out_specs=(
                columns, columns, by_pair(LANES, length), row, whole((tokens, model)), whole((tokens, model)),
            ),
            scratch_shapes=[pltpu.VMEM((length, model), F32)],
            compiler_params=params(60),
            cost_estimate=cost(7.5e+09, 6e+06),
        name="attend_back",
        )(k_r, v_r, kt_r, queries, qmark, kmark[r], dos, lse, delta, weights, weights, *dqt)
        dqt = (acc,)
        dkv[r] = (dk_r, dv_r)
        gbv = gbv_r if gbv is None else gbv + gbv_r
        arrived_x.append(swap(dxb, "tensor"))
        part = add(dxa, arrived_x[-1])
        if r == 0:
            own_part = part
        else:
            arrived.append(shift(part.astype(BF), -r, ctx))

    dq_all = after(dqt[0], up_terms[-1], arrived[0])
    down_terms = send_half([down_terms[0], after(down_terms[1], up_terms[-1])], down_order[0])
    up_terms = send_half(up_terms, up_order[1])
    lay_qkv = scatter_layout(ctx, rows, qkv_order, 1)
    piece = sds((2, 2, 3, ctx * rows, owidth), BF)
    dxq, gbq, qkv0, qkv1 = pl.pallas_call(
        lambda *refs: last_kernel(ctx, rows, lay_qkv, scale, *refs),
        grid=(quads,),
        out_shape=(sds((tokens, model), F32), sds((1, model), F32), piece, piece),
        in_specs=[scalars(), by_pair(LANES, length), of_kind(0)]
        + [whole((tokens, model))] * (2 * ctx) + [columns] * (2 * ctx),
        out_specs=(whole((tokens, model)), row, anywhere(), anywhere()),
        scratch_shapes=[
            pltpu.VMEM((3, model, model), BF), pltpu.VMEM((2 * ctx, model, tokens), BF),
            pltpu.VMEM((tokens, model), F32), pltpu.SemaphoreType.DMA((n_pieces,)),
        ],
        compiler_params=params(60),
        cost_estimate=cost(1.2e+10, 1.4e+07),
        name="last",
    )(ids, dq_all, weights, *[v for pair in zip(ring, sides) for v in pair],
      *[d[0] for d in dkv], *[d[1] for d in dkv])

    grad_in = dz1 + dxq + own_part
    for v in arrived:
        grad_in = grad_in + v.astype(F32)
    qkv_terms = [qkv0, swap(after(qkv1, down_terms[2]), "core")]
    qkv_terms = send_half(send_half(qkv_terms, qkv_order[0]), qkv_order[1])
    down_terms = send_half(down_terms, down_order[1])
    grad_up = send_line(up_terms, ctx, rows, 0)
    grad_down = send_line(down_terms, ctx, rows, 0)
    grad_qkv = send_line(qkv_terms, ctx, rows, 1).transpose(1, 0, 2)

    vectors = jnp.concatenate([gbq[0], gbv[0], vgrads.reshape(-1), gup_bias[0]])
    vectors = sum_everywhere(after(vectors.reshape(-1, LANES), qkv_terms[2]), ctx).reshape(-1)
    pick = lambda i: vectors[i * model : (i + 1) * model]
    part_of = lambda v, w: lax.dynamic_slice_in_dim(v, t * w, w)
    grad_bqv = jnp.stack([part_of(pick(0), owidth), part_of(pick(1), owidth)])

    return (
        result,
        both_halves(grad_in.astype(BF)).astype(F32),
        grad_qkv,
        grad_bqv,
        grad_down[:, width:],
        pick(2),
        pick(3),
        pick(4),
        grad_up,
        part_of(vectors[10 * model :], width),
        grad_down[:, :width],
        pick(5),
        pick(6),
        pick(7),
    )


neg_large = -1e30


def general_norm(summed, gain, bias):
    centred = summed - jnp.mean(summed, -1, keepdims=True)
    scaling = lax.rsqrt(jnp.mean(centred * centred, -1, keepdims=True) + 1e-05)
    normal_part = centred * scaling
    return (normal_part * gain + bias, normal_part, scaling)


def general_back(upstream, normal_part, scaling, gain):
    scaled = upstream * gain
    inner = (
        scaled
        - jnp.mean(scaled, -1, keepdims=True)
        - normal_part * jnp.mean(scaled * normal_part, -1, keepdims=True)
    )
    return (inner * scaling, jnp.sum(upstream * normal_part, 0), jnp.sum(upstream, 0))


def gelu_exact(inputs):
    return 0.5 * inputs * (1.0 + lax.erf(inputs * 0.7071067811865476))


def gelu_slope(inputs):
    return (
        0.5 * (1.0 + lax.erf(inputs * 0.7071067811865476))
        + inputs * jnp.exp(-0.5 * inputs * inputs) * 0.3989422804014327
    )


def general(
    layer_input,
    segments,
    w_qkv,
    b_qv,
    w_out,
    b_out,
    ln1_gain,
    ln1_bias,
    w_up,
    b_up,
    w_down,
    b_down,
    ln2_gain,
    ln2_bias,
    cotangent,
):
    inputs = layer_input[0]
    tokens = inputs.shape[0]
    group_len = tokens * lax.axis_size("ctx")
    seg_all = segments[0]
    seg_query = lax.dynamic_slice_in_dim(seg_all, lax.axis_index("ctx") * tokens, tokens)
    qkv_full, out_full, up_full, down_full = (
        lax.all_gather(w_qkv, ("shard", "ctx"), axis=0, tiled=True),
        lax.all_gather(w_out, ("shard", "ctx"), axis=0, tiled=True),
        lax.all_gather(w_up, ("shard", "ctx"), axis=0, tiled=True),
        lax.all_gather(w_down, ("shard", "ctx"), axis=0, tiled=True),
    )
    local_width = qkv_full.shape[2]
    heads_here = local_width // HD
    projected = jnp.einsum("td,dwe->wte", inputs, qkv_full, preferred_element_type=jnp.float32)
    bias_pair = b_qv.astype(jnp.float32)
    queries = (projected[0] + bias_pair[0]).astype(jnp.bfloat16)
    key_rows = projected[1].astype(jnp.bfloat16)
    value_rows = (projected[2] + bias_pair[1]).astype(jnp.bfloat16)
    keys_all, values_all = (
        lax.all_gather(key_rows, "ctx", axis=0, tiled=True),
        lax.all_gather(value_rows, "ctx", axis=0, tiled=True),
    )
    query_heads = queries.reshape(tokens, heads_here, HD).transpose(1, 0, 2)
    width_block = min(512, group_len)
    count_blocks = group_len // width_block
    key_blocks = keys_all.reshape(count_blocks, width_block, heads_here, HD)
    value_blocks = values_all.reshape(count_blocks, width_block, heads_here, HD)
    seg_blocks = seg_all.reshape(count_blocks, width_block)

    def scores_of(key_block, seg_block):
        raw = 0.125 * jnp.einsum(
            "htd,khd->htk", query_heads, key_block, preferred_element_type=jnp.float32
        )
        return jnp.where((seg_query[:, None] == seg_block[None, :])[None], raw, neg_large)

    def running_stats(carry, element):
        top_now, mass = carry
        scores = scores_of(element[0], element[1])
        top_next = jnp.maximum(top_now, jnp.max(scores, -1))
        mass = mass * jnp.exp(top_now - top_next) + jnp.sum(
            jnp.exp(scores - top_next[..., None]), -1
        )
        return ((top_next, mass), None)

    start_top = jnp.full((heads_here, tokens), neg_large, jnp.float32)
    (top_final, mass_final), unused = lax.scan(
        running_stats, (start_top, jnp.zeros_like(start_top)), (key_blocks, seg_blocks)
    )
    log_mass = top_final + jnp.log(mass_final)

    def mix_values(accum, element):
        probs = jnp.exp(scores_of(element[0], element[2]) - log_mass[..., None]).astype(
            jnp.bfloat16
        )
        return (
            accum
            + jnp.einsum("htk,khd->htd", probs, element[1], preferred_element_type=jnp.float32),
            None,
        )

    blocks_all = (key_blocks, value_blocks, seg_blocks)
    attended, unused = lax.scan(
        mix_values, jnp.zeros((heads_here, tokens, HD), jnp.float32), blocks_all
    )
    attended_rows = attended.transpose(1, 0, 2).reshape(tokens, local_width).astype(jnp.bfloat16)
    branch_part = jnp.einsum(
        "te,de->td", attended_rows, out_full, preferred_element_type=jnp.float32
    )
    branch = lax.psum(branch_part.astype(jnp.bfloat16), "tensor").astype(
        jnp.float32
    ) + b_out.astype(jnp.float32)
    first_gain = ln1_gain.astype(jnp.float32)
    second_gain = ln2_gain.astype(jnp.float32)
    hidden, first_normal, first_scale = general_norm(
        inputs.astype(jnp.float32) + branch, first_gain, ln1_bias.astype(jnp.float32)
    )
    hidden_low = hidden.astype(jnp.bfloat16)
    pre_act = jnp.dot(hidden_low, up_full, preferred_element_type=jnp.float32) + b_up.astype(
        jnp.float32
    )
    activated = gelu_exact(pre_act).astype(jnp.bfloat16)
    second_part = jnp.einsum("tf,df->td", activated, down_full, preferred_element_type=jnp.float32)
    second_branch = lax.psum(second_part.astype(jnp.bfloat16), "tensor").astype(
        jnp.float32
    ) + b_down.astype(jnp.float32)
    result, second_normal, second_scale = general_norm(
        hidden + second_branch, second_gain, ln2_bias.astype(jnp.float32)
    )
    qkv_full, out_full, up_full, down_full = (
        lax.all_gather(w_qkv, ("shard", "ctx"), axis=0, tiled=True),
        lax.all_gather(w_out, ("shard", "ctx"), axis=0, tiled=True),
        lax.all_gather(w_up, ("shard", "ctx"), axis=0, tiled=True),
        lax.all_gather(w_down, ("shard", "ctx"), axis=0, tiled=True),
    )
    upstream = cotangent[0].astype(jnp.float32)
    second_grad, grad_gain_two, grad_bias_two = general_back(
        upstream, second_normal, second_scale, second_gain
    )
    grad_down_bias = jnp.sum(second_grad, 0)
    second_low = second_grad.astype(jnp.bfloat16)
    grad_down = jnp.einsum("td,tf->df", second_low, activated, preferred_element_type=jnp.float32)
    act_grad = jnp.einsum("td,df->tf", second_low, down_full, preferred_element_type=jnp.float32)
    pre_grad = act_grad * gelu_slope(pre_act)
    grad_up_bias = jnp.sum(pre_grad, 0)
    pre_low = pre_grad.astype(jnp.bfloat16)
    grad_up = jnp.einsum("td,tf->df", hidden_low, pre_low, preferred_element_type=jnp.float32)
    hidden_part = jnp.einsum("tf,df->td", pre_low, up_full, preferred_element_type=jnp.float32)
    hidden_grad = second_grad + lax.psum(hidden_part.astype(jnp.bfloat16), "tensor").astype(
        jnp.float32
    )
    first_grad, grad_gain_one, grad_bias_one = general_back(
        hidden_grad, first_normal, first_scale, first_gain
    )
    grad_out_bias = jnp.sum(first_grad, 0)
    first_low = first_grad.astype(jnp.bfloat16)
    grad_out = jnp.einsum("td,te->de", first_low, attended_rows, preferred_element_type=jnp.float32)
    attended_grad = jnp.einsum(
        "td,de->te", first_low, out_full, preferred_element_type=jnp.float32
    ).astype(jnp.bfloat16)
    grad_heads = attended_grad.reshape(tokens, heads_here, HD).transpose(1, 0, 2)
    row_delta = jnp.sum(grad_heads.astype(jnp.float32) * attended, -1)

    def prob_pair(element):
        probs = jnp.exp(scores_of(element[0], element[2]) - log_mass[..., None])
        prob_grad = jnp.einsum(
            "htd,khd->htk", grad_heads, element[1], preferred_element_type=jnp.float32
        )
        return (probs, prob_grad)

    zero_heads = jnp.zeros((heads_here, tokens, HD), jnp.float32)

    def score_grads(accum, element):
        probs, prob_grad = prob_pair(element)
        score_grad = (probs * (prob_grad - row_delta[..., None])).astype(jnp.bfloat16)
        accum = accum + 0.125 * jnp.einsum(
            "htk,khd->htd", score_grad, element[0], preferred_element_type=jnp.float32
        )
        key_grad = 0.125 * jnp.einsum(
            "htk,htd->khd", score_grad, query_heads, preferred_element_type=jnp.float32
        )
        value_grad = jnp.einsum(
            "htk,htd->khd",
            probs.astype(jnp.bfloat16),
            grad_heads,
            preferred_element_type=jnp.float32,
        )
        return (accum, (key_grad, value_grad))

    query_grad, (key_parts, value_parts) = lax.scan(score_grads, zero_heads, blocks_all)
    key_sum, value_sum = (
        lax.psum_scatter(
            key_parts.reshape(group_len, local_width).astype(jnp.bfloat16),
            "ctx",
            scatter_dimension=0,
            tiled=True,
        ).astype(jnp.float32),
        lax.psum_scatter(
            value_parts.reshape(group_len, local_width).astype(jnp.bfloat16),
            "ctx",
            scatter_dimension=0,
            tiled=True,
        ).astype(jnp.float32),
    )
    query_rows = query_grad.transpose(1, 0, 2).reshape(tokens, local_width)
    bias_grads = jnp.stack([jnp.sum(query_rows, 0), jnp.sum(value_sum, 0)])
    stacked = jnp.stack([query_rows, key_sum, value_sum]).astype(jnp.bfloat16)
    grad_qkv = jnp.einsum("td,wte->dwe", inputs, stacked, preferred_element_type=jnp.float32)
    input_part = jnp.einsum("wte,dwe->td", stacked, qkv_full, preferred_element_type=jnp.float32)
    grad_inputs = first_grad + lax.psum(input_part.astype(jnp.bfloat16), "tensor").astype(
        jnp.float32
    )
    matrices = (
        lax.psum_scatter(grad_qkv, ("shard", "ctx"), scatter_dimension=0, tiled=True),
        lax.psum_scatter(grad_out, ("shard", "ctx"), scatter_dimension=0, tiled=True),
        lax.psum_scatter(grad_up, ("shard", "ctx"), scatter_dimension=0, tiled=True),
        lax.psum_scatter(grad_down, ("shard", "ctx"), scatter_dimension=0, tiled=True),
    )
    vectors = lax.psum(
        (
            bias_grads,
            grad_out_bias,
            grad_gain_one,
            grad_bias_one,
            grad_up_bias,
            grad_down_bias,
            grad_gain_two,
            grad_bias_two,
        ),
        ("shard", "ctx"),
    )
    return (
        result.astype(jnp.bfloat16)[None],
        grad_inputs[None],
        matrices[0],
        vectors[0],
        matrices[1],
        vectors[1],
        vectors[2],
        vectors[3],
        matrices[2],
        vectors[4],
        matrices[3],
        vectors[5],
        vectors[6],
        vectors[7],
    )


def solution(mesh):
    sizes = dict(mesh.shape)
    ctx = sizes["ctx"]
    fits = sizes["shard"] == 4 and sizes["tensor"] == 2 and ctx & (ctx - 1) == 0
    if fits:
        mesh = Mesh(mesh.devices.reshape(2, 2, ctx, 2), EVERY)
        shard, body = ("y", "core"), on_device
        rows = ("y", "core", "ctx")
    else:
        shard, body = "shard", general
        rows = ("shard", "ctx")
    activations, matrix = P(shard, "ctx", None), P(rows, "tensor")
    cube, pair = P(rows, None, "tensor"), P(None, "tensor")
    return jax.shard_map(
        body,
        mesh=mesh,
        in_specs=(
            activations, P(shard, None), cube, pair, matrix, P(), P(), P(), matrix, P("tensor"),
            matrix, P(), P(), P(), activations,
        ),
        out_specs=(
            activations, activations, cube, pair, matrix, P(), P(), P(), matrix, P("tensor"),
            matrix, P(), P(), P(),
        ),
        check_vma=False,
    )
```

```python
import math

import jax
import jax.numpy as jnp
from jax import lax
from jax.experimental import pallas as pl
from jax.experimental.pallas import tpu as pltpu
from jax.sharding import Mesh
from jax.sharding import PartitionSpec as P

HD = 64
LANES = 128
BF = jnp.bfloat16
F32 = jnp.float32
NT = (((1,), (1,)), ((), ()))
NN = (((1,), (0,)), ((), ()))
EVERY = ("y", "core", "ctx", "tensor")
SWAP = ((0, 1), (1, 0))


def mm(a, b, dims=NN):
    return lax.dot_general(a, b, dims, preferred_element_type=F32)


def cost(flops, size):
    return pl.CostEstimate(flops=int(flops * 0.4), bytes_accessed=int(size * 0.4), transcendentals=0)


def params(mib):
    return pltpu.CompilerParams(vmem_limit_bytes=mib << 20)


def anywhere():
    return pl.BlockSpec(memory_space=pl.ANY)


def whole(shape):
    return pl.BlockSpec(shape, lambda *_: (0,) * len(shape))


def scalars():
    return pl.BlockSpec(memory_space=pltpu.SMEM)


def owner_of(ids, piece, ctx):
    rc, ry, rx, rz = piece
    y = (ids[0] + ry) % 2
    core = (ids[1] + rc) % 2
    place = (ids[2] + (ctx - rz)) % ctx
    return (y * 2 + core) * ctx + place, (ids[3] + rx) % 2


def piece_copies(ids, refs, layout, full, sem, ctx, rows, width, back=False, base=0):
    copies = []
    for ref, pieces, at in zip(refs, layout, range(len(refs))):
        for index, piece in pieces:
            block, half = piece if len(piece) == 2 else owner_of(ids, piece, ctx)
            row, column = block * rows, half * width
            if len(piece) > 2:
                row, column = pl.multiple_of(row, 16), pl.multiple_of(column, LANES)
            if len(full.shape) == 3:
                there = full.at[:, pl.ds(row, rows), pl.ds(column, width)]
            else:
                there = full.at[pl.ds(row, rows), pl.ds(column, width)]
            here = ref.at[index]
            source, target = (there, here) if back else (here, there)
            copies.append(pltpu.make_async_copy(source, target, sem.at[base + len(copies)]))
    return copies


def prepare_kernel(ctx, rows, width, layout, n, heads, scale, ids, xt, bq, *rest):
    pieces, (weights, queries, sem) = rest[:n], rest[n:]
    copies = piece_copies(ids, pieces, layout, weights, sem, ctx, rows, width)
    for copy in copies:
        copy.start()
    for copy in copies:
        copy.wait()
    tokens = xt.shape[0]
    lane = lax.broadcasted_iota(jnp.int32, (tokens, LANES), 1)
    projected = mm(xt[...], weights[0]) + bq[...]
    projected = (projected.astype(BF).astype(F32) * scale)
    for pair in range(heads // 2):
        two = projected[:, pair * LANES : (pair + 1) * LANES]
        even = jnp.where(lane < HD, two, 0.0).astype(BF)
        odd = jnp.where(lane >= HD, two, 0.0).astype(BF)
        queries[pair] = jnp.concatenate([even, odd], 0)


def attend_kernel(first, xa, xb, wk, wv, bv, queries, qmark, kmark, *rest):
    if first:
        keys, values, keys_t, top_out, sums_out = rest
    else:
        top_in, sums_in, keys, values, keys_t, top_out, sums_out = rest
    x = jnp.concatenate([xa[...], xb[...]], 0)
    k4 = mm(x, wk[...]).astype(BF)
    v4 = mm(x, wv[...]) + bv[...]
    keys[...] = k4
    values[...] = v4.astype(BF)
    keys_t[...] = k4.T
    v4t = v4.T.astype(BF)
    ones = jnp.ones((16, x.shape[0]), BF)
    for j in range(2):
        span = slice(j * LANES, (j + 1) * LANES)
        kk = jnp.concatenate([k4[:, span], kmark[...]], 1)
        qq = jnp.concatenate([queries[j], qmark[...]], 1)
        scores = mm(kk, qq, NT)
        top = jnp.max(scores, 0, keepdims=True)
        if not first:
            top = jnp.maximum(top, top_in[j])
        probs = jnp.exp(scores - top).astype(BF)
        sums = mm(jnp.concatenate([v4t[span], ones], 0), probs)
        if not first:
            sums = sums + sums_in[j] * jnp.exp(top_in[j] - top)
        top_out[j] = top
        sums_out[j] = sums


def normed(z, eps=1e-05):
    centred = z - jnp.mean(z, -1, keepdims=True)
    factor = lax.rsqrt(jnp.mean(centred * centred, -1, keepdims=True) + eps)
    return centred * factor, factor


def norm_back(e, n, factor, gain):
    scaled = e * gain
    return factor * (
        scaled - jnp.mean(scaled, -1, keepdims=True) - n * jnp.mean(scaled * n, -1, keepdims=True)
    )


def total(v):
    return jnp.sum(v, 0, keepdims=True)


def middle_kernel(ctx, rows, lay_up, lay_down, lay_out, n, heads, ids, sums, top, xt, cot, vec, b_up, *rest):
    feeds, rest = rest[:n], rest[n:]
    (
        out_ref, dz1_ref, dos, lse, delta, vgrads, gup_bias,
        u_ref, dpb_ref, h1b_ref, dmb_ref, dzb_ref, ob_ref,
        wup, wdown, wout, pre_s, prod, sem_up, sem_down, sem_out,
    ) = rest
    width = wup.shape[1] // 2
    owidth = wout.shape[1] // 2
    up_part, out_part, down_part = (
        [d.at[:, a:b] for d in feeds]
        for a, b in ((0, width), (width, width + owidth), (width + owidth, 2 * width + owidth))
    )
    c_out = piece_copies(ids, out_part, lay_out, wout, sem_out, ctx, rows, owidth)
    c_up = piece_copies(ids, up_part, lay_up, wup, sem_up, ctx, rows, width)
    c_down = piece_copies(ids, down_part, lay_down, wdown, sem_down, ctx, rows, width)
    for copy in c_out + c_up + c_down:
        copy.start()
    tokens, model = xt.shape
    pairs = heads // 2
    half = tokens
    parts = []
    for p in range(pairs):
        mass = sums[p, LANES : LANES + 1, :]
        ot = sums[p, 0:LANES, :] / mass
        lse[p] = top[p] + jnp.log(mass)
        parts.append(jnp.concatenate([ot[0:HD, 0:half], ot[HD:LANES, half : 2 * half]], 0).T)
    o = jnp.concatenate(parts, 1)
    ob = o.astype(BF)
    ob_ref[...] = ob
    for copy in c_out:
        copy.wait()
    b_out, g1, b1, b_down, g2, b2 = (vec[i : i + 1, :] for i in range(6))
    z1 = xt[...].astype(F32) + mm(ob, wout[...], NT) + b_out
    n1, f1 = normed(z1)
    h1 = n1 * g1 + b1
    h1b = h1.astype(BF)
    h1b_ref[...] = h1b
    for copy in c_up:
        copy.wait()
    hidden = wup.shape[1]
    step = model
    for c in range(0, hidden, step):
        pre = mm(h1b, wup[:, c : c + step]) + b_up[:, c : c + step]
        pre_s[:, c : c + step] = pre
        u_ref[:, c : c + step] = (0.5 * pre * (1.0 + lax.erf(pre * 0.7071067811865476))).astype(BF)
    for copy in c_down:
        copy.wait()
    m = mm(u_ref[...], wdown[...], NT) + b_down
    n2, f2 = normed(h1 + m)
    out_ref[...] = (n2 * g2 + b2).astype(BF)
    g = cot[...].astype(F32)
    dz2 = norm_back(g, n2, f2, g2)
    dmb = dz2.astype(BF)
    dmb_ref[...] = dmb
    vgrads[3:4, :] = total(dz2)
    vgrads[4:5, :] = total(g * n2)
    vgrads[5:6, :] = total(g)
    for c in range(0, hidden, step):
        pre = pre_s[:, c : c + step]
        slope = 0.5 * (1.0 + lax.erf(pre * 0.7071067811865476)) + pre * jnp.exp(
            -0.5 * pre * pre
        ) * 0.3989422804014327
        dpre = mm(dmb, wdown[:, c : c + step]) * slope
        gup_bias[:, c : c + step] = total(dpre)
        dpb_ref[:, c : c + step] = dpre.astype(BF)
    dh1 = dz2 + mm(dpb_ref[...], wup[...], NT)
    dz1 = norm_back(dh1, n1, f1, g1)
    dz1_ref[...] = dz1
    vgrads[0:1, :] = total(dz1)
    vgrads[1:2, :] = total(dh1 * n1)
    vgrads[2:3, :] = total(dh1)
    vgrads[6:8, :] = jnp.zeros((2, model), F32)
    dzb = dz1.astype(BF)
    dzb_ref[...] = dzb
    do = mm(dzb, wout[...]).astype(BF).astype(F32)
    prod[...] = do * o
    spread = (
        lax.broadcasted_iota(jnp.int32, (16, model), 1) // HD
        == lax.broadcasted_iota(jnp.int32, (16, model), 0)
    ).astype(F32)
    by_head = lax.dot_general(
        spread, prod[...], NT, precision=lax.Precision.HIGHEST, preferred_element_type=F32
    )
    lane = lax.broadcasted_iota(jnp.int32, (tokens, LANES), 1)
    for p in range(pairs):
        two = do[:, p * LANES : (p + 1) * LANES]
        dos[p] = jnp.concatenate(
            [jnp.where(lane < HD, two, 0.0).astype(BF), jnp.where(lane >= HD, two, 0.0).astype(BF)], 0
        )
        delta[p] = jnp.concatenate([by_head[2 * p : 2 * p + 1], by_head[2 * p + 1 : 2 * p + 2]], 1)


def feed_grads_kernel(ctx, rows, lay_up, lay_down, lay_out, ids, h1b, dmb, dzb, ob, u, dpb,
                      up0, up1, down0, down1, gup, gdown, gout, h1t, dmt, sem_up, sem_down, sem_out):
    step = pl.program_id(0)
    model = gup.shape[0]
    width, owidth = gup.shape[1] // 2, gout.shape[1] // 2

    @pl.when(step == 0)
    def _():
        h1t[...] = h1b[...].T
        dmt[...] = dmb[...].T
        gout[...] = mm(dzb[...].T, ob[...]).astype(BF)

    span = pl.ds(pl.multiple_of(step * model, LANES), model)
    gup[:, span] = mm(h1t[...], dpb[...]).astype(BF)
    gdown[:, span] = mm(dmt[...], u[...]).astype(BF)

    @pl.when(step == pl.num_programs(0) - 1)
    def _():
        downs = [down0, down1]
        copies = piece_copies(ids, [up0, up1], lay_up, gup, sem_up, ctx, rows, width, True)
        copies += piece_copies(
            ids, [d.at[..., 0:width] for d in downs], lay_down, gdown, sem_down, ctx, rows, width, True)
        copies += piece_copies(
            ids, [d.at[..., width : width + owidth] for d in downs], lay_out, gout, sem_out, ctx, rows, owidth, True)
        for copy in copies:
            copy.start()
        for copy in copies:
            copy.wait()


def attend_back_kernel(first, keys, values, keys_t, queries, qmark, kmark, dos, lse, delta, wk, wv, *rest):
    if first:
        dk_ref, dv_ref, dqt_out, gbv, dxa, dxb, dx = rest
    else:
        dqt_in, dk_ref, dv_ref, dqt_out, gbv, dxa, dxb, dx = rest
    step = pl.program_id(0)
    k4, v4 = keys[...], values[...]
    dks, dvs = [], []
    for j in range(2):
        span = slice(j * LANES, (j + 1) * LANES)
        kk = jnp.concatenate([k4[:, span], kmark[...]], 1)
        qq = jnp.concatenate([queries[j], qmark[...]], 1)
        probs = jnp.exp(mm(kk, qq, NT) - lse[j])
        ds = (probs * (mm(v4[:, span], dos[j], NT) - delta[j])).astype(BF)
        dvs.append(mm(probs.astype(BF), dos[j]))
        dks.append(mm(ds, queries[j]))
        dqt = mm(keys_t[span], ds)
        dqt_out[j] = dqt if first else dqt_in[j] + dqt
    dv4 = jnp.concatenate(dvs, 1)
    gbv[...] = total(dv4)
    dkb, dvb = jnp.concatenate(dks, 1).astype(BF), dv4.astype(BF)
    dk_ref[...] = dkb
    dv_ref[...] = dvb
    part = mm(dkb, wk[...], NT) + mm(dvb, wv[...], NT)

    @pl.when(step == 0)
    def _():
        dx[...] = part

    @pl.when(step > 0)
    def _():
        dx[...] += part

    @pl.when(step == pl.num_programs(0) - 1)
    def _():
        half = dxa.shape[0]
        dxa[...] = dx[0:half].astype(BF)
        dxb[...] = dx[half:].astype(BF)


def last_kernel(ctx, rows, layout, scale, ids, dqt, wq, *rest):
    blocks = 2 * ctx
    xs, rest = rest[:blocks], rest[blocks:]
    dks, rest = rest[:ctx], rest[ctx:]
    dvs, rest = rest[:ctx], rest[ctx:]
    dxq, gbq, out0, out1, grads, xts, dx, sem = rest
    step = pl.program_id(0)
    half = xs[0].shape[0]

    @pl.when(step == 0)
    def _():
        for i in range(blocks):
            xts[i] = xs[i][...].T

    cols = []
    for j in range(2):
        t = dqt[j]
        cols.append(jnp.concatenate([t[0:HD, 0:half], t[HD:LANES, half : 2 * half]], 0).T)
    dq = jnp.concatenate(cols, 1) * scale
    gbq[...] = total(dq)
    dqb = dq.astype(BF)
    width = dqb.shape[1]
    span = pl.ds(pl.multiple_of(step * width, LANES), width)
    part = mm(dqb, wq[...], NT)

    @pl.when(step == 0)
    def _():
        dx[...] = part

    @pl.when(step > 0)
    def _():
        dx[...] += part

    grads[0, :, span] = mm(xts[0], dqb).astype(BF)
    for kind, parts in ((1, dks), (2, dvs)):
        acc = None
        for r in range(ctx):
            for side in range(2):
                one = mm(xts[2 * r + side], parts[r][side * half : (side + 1) * half, :])
                acc = one if acc is None else acc + one
        grads[kind, :, span] = acc.astype(BF)

    @pl.when(step == pl.num_programs(0) - 1)
    def _():
        dxq[...] = dx[...]
        copies = piece_copies(ids, [out0, out1], layout, grads, sem, ctx, rows, grads.shape[2] // 2, True)
        for copy in copies:
            copy.start()
        for copy in copies:
            copy.wait()


def shift(v, by, ctx):
    return lax.ppermute(v, "ctx", [(i, (i + by) % ctx) for i in range(ctx)])


def swap(v, axis):
    return lax.ppermute(v, axis, SWAP)


def after(v, *done):
    return lax.optimization_barrier((v,) + done)[0]


def spread_pieces(line, ctx, rows, order, axis):
    both = jnp.concatenate([line, swap(line, order[0])], axis)
    far = swap(both, order[1])
    arrays, layout = [], []
    for rc in range(2):
        for second, v in ((0, both), (1, far)):
            arrays.append(v if rc == 0 else swap(v, "core"))
            pieces = []
            for first in range(2):
                for rz in range(ctx):
                    at = (first * ctx + rz) * rows
                    index = (slice(None),) * axis + (slice(at, at + rows),)
                    rel = {order[0]: first, order[1]: second}
                    pieces.append((index, (rc, rel["y"], rel["tensor"], rz)))
            layout.append(pieces)
    return arrays, layout


def spread_square(line, ctx, rows, axis):
    over_x, over_y = swap(line, "tensor"), swap(line, "y")
    over_both = swap(over_x, "y")
    arrays, layout = [], []
    for rx, ry, v in ((0, 0, line), (1, 0, over_x), (0, 1, over_y), (1, 1, over_both)):
        for rc in range(2):
            arrays.append(v if rc == 0 else swap(v, "core"))
            layout.append([
                ((slice(None),) * axis + (slice(rz * rows, (rz + 1) * rows),), (rc, ry, rx, rz))
                for rz in range(ctx)
            ])
    return arrays, layout


def scatter_layout(ctx, rows, order, lead):
    layout = []
    for rc in range(2):
        pieces = []
        for first in range(2):
            for second in range(2):
                for rz in range(ctx):
                    rel = {order[0]: first, order[1]: second}
                    index = (first, second) + (slice(None),) * lead + (slice(rz * rows, (rz + 1) * rows),)
                    pieces.append((index, (rc, rel["y"], rel["tensor"], rz)))
        layout.append(pieces)
    return layout


def add(a, b):
    return a.astype(F32) + b.astype(F32)


def send_half(terms, axis):
    sent = terms[0][1].astype(F32)
    for v in terms[1:]:
        sent = sent + v[1].astype(F32)
    return [v[0] for v in terms] + [swap(sent.astype(BF), axis)]


def send_line(terms, ctx, rows, axis):
    cut = lambda v, r: lax.slice_in_dim(v, r * rows, (r + 1) * rows, axis=axis).astype(F32)
    sums = [sum(cut(v, r) for v in terms) for r in range(ctx)]
    result = sums[0]
    for r in range(1, ctx):
        result = result + shift(sums[r].astype(BF), -r, ctx).astype(F32)
    return result


def sum_everywhere(v, ctx):
    for axis in ("core", "tensor", "y"):
        v = v + swap(v, axis)
    bit = 1
    while bit < ctx:
        v = v + lax.ppermute(v, "ctx", [(i, i ^ bit) for i in range(ctx)])
        bit *= 2
    return v


def on_device(
    layer_input, segments, w_qkv, b_qv, w_out, b_out, ln1_gain, ln1_bias,
    w_up, b_up, w_down, b_down, ln2_gain, ln2_bias, cotangent,
):
    ctx = lax.axis_size("ctx")
    y, core, z, t = (lax.axis_index(a) for a in EVERY)
    ids = jnp.stack([y, core, z, t]).astype(jnp.int32)
    x = layer_input[0]
    tokens = x.shape[0] // 2
    model = x.shape[1]
    heads = model // HD
    pairs = heads // 2
    quads = heads // 4
    quad = 4 * HD
    rows, width, owidth = w_up.shape[0], w_up.shape[1], w_out.shape[1]
    hidden = 2 * width
    length = 2 * tokens
    scale = 1.0 / math.sqrt(HD)

    own = lambda v: lax.dynamic_slice_in_dim(v, t * tokens, tokens)
    other = lambda v: lax.dynamic_slice_in_dim(v, (1 - t) * tokens, tokens)
    xt = own(x)

    w_local = w_qkv.transpose(1, 0, 2)
    q_line = jnp.concatenate([w_local] + [shift(w_local, r, ctx) for r in range(1, ctx)], 1)
    wq_arrays, wq_layout = spread_square(q_line, ctx, rows, 1)
    feed = lax.all_gather(jnp.concatenate([w_up, w_out, w_down], 1), EVERY, axis=0, tiled=True)
    feed_layout = [[
        ((slice(k * rows, (k + 1) * rows),), (k // 2, k % 2)) for k in range(8 * ctx)
    ]]
    ring = [xt]
    for _ in range(1, ctx):
        ring.append(shift(ring[-1], 1, ctx))
    sides = [other(x)] + [swap(v, "tensor") for v in ring[1:]]
    seg = segments[0].reshape(ctx, 2, tokens)[::-1]
    seg = lax.dynamic_slice_in_dim(jnp.concatenate([seg, seg]), ctx - 1 - z, ctx)
    seg = jnp.where(t == 0, seg, seg[:, ::-1])
    mark = jnp.arange(LANES, dtype=jnp.int32)
    kmark = jnp.where(
        (mark < 3) & (seg.reshape(ctx, length)[..., None] != mark), -1e30, 0.0
    ).astype(BF)
    qmark = (seg[0, 0][:, None] == mark).astype(BF)
    qmark = jnp.concatenate([qmark, qmark])

    mine = jnp.concatenate([b_qv.reshape(1, -1), b_up.reshape(1, -1)], 1)
    mine = jnp.concatenate([mine, jnp.zeros_like(mine)]).astype(F32)
    theirs = swap(mine, "tensor")
    lower, upper = jnp.where(t == 0, mine, theirs)[:1], jnp.where(t == 0, theirs, mine)[:1]
    cut = lambda a, b: jnp.concatenate([lower[:, a:b], upper[:, a:b]], 1)
    biases = jnp.concatenate([cut(0, owidth), cut(owidth, 2 * owidth)])
    bup_full = cut(2 * owidth, 2 * owidth + width)

    n_pieces = 4 * ctx * 2
    weights, queries = pl.pallas_call(
        lambda *refs: prepare_kernel(ctx, rows, owidth, wq_layout, 8, heads, scale, *refs),
        out_shape=(
            jax.ShapeDtypeStruct((3, model, model), BF),
            jax.ShapeDtypeStruct((pairs, length, LANES), BF),
        ),
        in_specs=[scalars(), whole((tokens, model)), whole((1, model))] + [anywhere()] * 8,
        out_specs=(whole((3, model, model)), whole((pairs, length, LANES))),
        scratch_shapes=[pltpu.SemaphoreType.DMA((n_pieces,))],
        compiler_params=params(60),
        cost_estimate=cost(3e+09, 5e+06),
        name="prepare",
    )(ids, xt, biases[0:1], *wq_arrays)

    def of_kind(kind):
        return pl.BlockSpec((None, model, quad), lambda g: (kind, 0, g))

    columns = pl.BlockSpec((length, quad), lambda g: (0, g))
    rows_t = pl.BlockSpec((quad, length), lambda g: (g, 0))
    row = pl.BlockSpec((1, quad), lambda g: (0, g))
    by_pair = lambda *tail: pl.BlockSpec((2,) + tail, lambda g: (g,) + (0,) * len(tail))

    kv = []
    carry = ()
    state_shapes = (
        jax.ShapeDtypeStruct((pairs, 1, length), F32),
        jax.ShapeDtypeStruct((pairs, LANES + 16, length), F32),
    )
    state_specs = (by_pair(1, length), by_pair(LANES + 16, length))
    for r in range(ctx):
        first = r == 0
        k_r, v_r, kt_r, *carry = pl.pallas_call(
            lambda *refs, first=first: attend_kernel(first, *refs),
            grid=(quads,),
            out_shape=(
                jax.ShapeDtypeStruct((length, model), BF),
                jax.ShapeDtypeStruct((length, model), BF),
                jax.ShapeDtypeStruct((model, length), BF),
            ) + state_shapes,
            in_specs=[
                whole((tokens, model)), whole((tokens, model)), of_kind(1), of_kind(2), row,
                by_pair(length, LANES), whole((length, LANES)), whole((length, LANES)),
            ] + ([] if first else list(state_specs)),
            out_specs=(columns, columns, rows_t) + state_specs,
            compiler_params=params(60),
            cost_estimate=cost(5.5e+09, 4e+06),
        name="attend",
        )(ring[r], sides[r], weights, weights, biases[1:2], queries, qmark, kmark[r], *carry)
        kv.append((k_r, v_r, kt_r))
    top, sums = carry

    vec = jnp.stack(
        [b_out, ln1_gain, ln1_bias, b_down, ln2_gain, ln2_bias, ln2_bias, ln2_bias]
    ).astype(F32)
    sds = jax.ShapeDtypeStruct
    mid_shapes = (
        sds((tokens, model), BF), sds((tokens, model), F32), sds((pairs, length, LANES), BF),
        sds((pairs, 1, length), F32), sds((pairs, 1, length), F32), sds((8, model), F32),
        sds((1, hidden), F32), sds((tokens, hidden), BF), sds((tokens, hidden), BF),
        sds((tokens, model), BF), sds((tokens, model), BF), sds((tokens, model), BF),
        sds((tokens, model), BF),
    )
    (out_own, dz1, dos, lse, delta, vgrads, gup_bias, u, dpb, h1b, dmb, dzb, ob) = pl.pallas_call(
        lambda *refs: middle_kernel(ctx, rows, feed_layout, feed_layout, feed_layout, 1, heads, *refs),
        out_shape=mid_shapes,
        in_specs=[
            scalars(), whole(sums.shape), whole(top.shape), whole((tokens, model)),
            whole((tokens, model)), whole((8, model)), whole((1, hidden)),
        ] + [anywhere()],
        out_specs=tuple(whole(s.shape) for s in mid_shapes),
        scratch_shapes=[
            pltpu.VMEM((model, hidden), BF), pltpu.VMEM((model, hidden), BF),
            pltpu.VMEM((model, model), BF), pltpu.VMEM((tokens, hidden), F32),
            pltpu.VMEM((tokens, model), F32),
            pltpu.SemaphoreType.DMA((n_pieces,)), pltpu.SemaphoreType.DMA((n_pieces,)),
            pltpu.SemaphoreType.DMA((n_pieces,)),
        ],
        compiler_params=params(60),
        cost_estimate=cost(1.6e+10, 1.6e+07),
        name="middle",
    )(ids, sums, top, xt, own(cotangent[0]), vec, bup_full, feed)

    up_order, down_order, qkv_order = ("y", "tensor"), ("y", "tensor"), ("y", "tensor")
    lay_up = scatter_layout(ctx, rows, up_order, 0)
    lay_down = scatter_layout(ctx, rows, down_order, 0)
    piece = lambda w: sds((2, 2, ctx * rows, w), BF)
    chunk = pl.BlockSpec((tokens, model), lambda c: (0, c))
    up0, up1, down0, down1 = pl.pallas_call(
        lambda *refs: feed_grads_kernel(ctx, rows, lay_up, lay_down, lay_down, *refs),
        grid=(hidden // model,),
        out_shape=(piece(width), piece(width), piece(width + owidth), piece(width + owidth)),
        in_specs=[scalars()] + [whole((tokens, model))] * 4 + [chunk, chunk],
        out_specs=(anywhere(),) * 4,
        scratch_shapes=[
            pltpu.VMEM((model, hidden), BF), pltpu.VMEM((model, hidden), BF),
            pltpu.VMEM((model, model), BF), pltpu.VMEM((model, tokens), BF),
            pltpu.VMEM((model, tokens), BF),
            pltpu.SemaphoreType.DMA((n_pieces,)), pltpu.SemaphoreType.DMA((n_pieces,)),
            pltpu.SemaphoreType.DMA((n_pieces,)),
        ],
        compiler_params=params(60),
        cost_estimate=cost(9e+09, 1.2e+07),
        name="feed_grads",
    )(ids, h1b, dmb, dzb, ob, u, dpb)
    up_terms = [up0, swap(up1, "core")]
    down_terms = [down0, swap(down1, "core")]

    def both_halves(mine):
        theirs = swap(mine, "tensor")
        return jnp.where(
            t == 0, jnp.concatenate([mine, theirs]), jnp.concatenate([theirs, mine])
        )[None]

    result = both_halves(out_own)

    dkv, gbv, arrived, arrived_x = [None] * ctx, None, [], []
    delta = after(delta, up1)
    dqt = ()
    own_part = None
    for i, r in enumerate(list(range(1, ctx)) + [0]):
        first = i == 0
        if i == 1:
            dos = after(dos, up_terms[-1], down_terms[-1])
            up_terms = send_half(up_terms, up_order[0])
        elif i > 1:
            dos = after(dos, arrived_x[-1], *((result,) if i == 2 else ()))
        k_r, v_r, kt_r = kv[r]
        dk_r, dv_r, acc, gbv_r, dxa, dxb = pl.pallas_call(
            lambda *refs, first=first: attend_back_kernel(first, *refs),
            grid=(quads,),
            out_shape=(
                sds((length, model), BF), sds((length, model), BF), sds((pairs, LANES, length), F32),
                sds((1, model), F32), sds((tokens, model), BF), sds((tokens, model), BF),
            ),
            in_specs=[
                columns, columns, rows_t, by_pair(length, LANES), whole((length, LANES)),
                whole((length, LANES)), by_pair(length, LANES), by_pair(1, length), by_pair(1, length),
                of_kind(1), of_kind(2),
            ] + ([] if first else [by_pair(LANES, length)]),
            out_specs=(
                columns, columns, by_pair(LANES, length), row, whole((tokens, model)), whole((tokens, model)),
            ),
            scratch_shapes=[pltpu.VMEM((length, model), F32)],
            compiler_params=params(60),
            cost_estimate=cost(7.5e+09, 6e+06),
        name="attend_back",
        )(k_r, v_r, kt_r, queries, qmark, kmark[r], dos, lse, delta, weights, weights, *dqt)
        dqt = (acc,)
        dkv[r] = (dk_r, dv_r)
        gbv = gbv_r if gbv is None else gbv + gbv_r
        arrived_x.append(swap(dxb, "tensor"))
        part = add(dxa, arrived_x[-1])
        if r == 0:
            own_part = part
        else:
            arrived.append(shift(part.astype(BF), -r, ctx))

    dq_all = after(dqt[0], up_terms[-1], arrived[0])
    down_terms = send_half([down_terms[0], after(down_terms[1], up_terms[-1])], down_order[0])
    up_terms = send_half(up_terms, up_order[1])
    lay_qkv = scatter_layout(ctx, rows, qkv_order, 1)
    piece = sds((2, 2, 3, ctx * rows, owidth), BF)
    dxq, gbq, qkv0, qkv1 = pl.pallas_call(
        lambda *refs: last_kernel(ctx, rows, lay_qkv, scale, *refs),
        grid=(quads,),
        out_shape=(sds((tokens, model), F32), sds((1, model), F32), piece, piece),
        in_specs=[scalars(), by_pair(LANES, length), of_kind(0)]
        + [whole((tokens, model))] * (2 * ctx) + [columns] * (2 * ctx),
        out_specs=(whole((tokens, model)), row, anywhere(), anywhere()),
        scratch_shapes=[
            pltpu.VMEM((3, model, model), BF), pltpu.VMEM((2 * ctx, model, tokens), BF),
            pltpu.VMEM((tokens, model), F32), pltpu.SemaphoreType.DMA((n_pieces,)),
        ],
        compiler_params=params(60),
        cost_estimate=cost(1.2e+10, 1.4e+07),
        name="last",
    )(ids, dq_all, weights, *[v for pair in zip(ring, sides) for v in pair],
      *[d[0] for d in dkv], *[d[1] for d in dkv])

    grad_in = dz1 + dxq + own_part
    for v in arrived:
        grad_in = grad_in + v.astype(F32)
    qkv_terms = [qkv0, swap(after(qkv1, down_terms[2]), "core")]
    qkv_terms = send_half(send_half(qkv_terms, qkv_order[0]), qkv_order[1])
    down_terms = send_half(down_terms, down_order[1])
    grad_up = send_line(up_terms, ctx, rows, 0)
    grad_down = send_line(down_terms, ctx, rows, 0)
    grad_qkv = send_line(qkv_terms, ctx, rows, 1).transpose(1, 0, 2)

    vectors = jnp.concatenate([gbq[0], gbv[0], vgrads.reshape(-1), gup_bias[0]])
    vectors = sum_everywhere(after(vectors.reshape(-1, LANES), qkv_terms[3]), ctx).reshape(-1)
    pick = lambda i: vectors[i * model : (i + 1) * model]
    part_of = lambda v, w: lax.dynamic_slice_in_dim(v, t * w, w)
    grad_bqv = jnp.stack([part_of(pick(0), owidth), part_of(pick(1), owidth)])

    return (
        result,
        both_halves(grad_in.astype(BF)).astype(F32),
        grad_qkv,
        grad_bqv,
        grad_down[:, width:],
        pick(2),
        pick(3),
        pick(4),
        grad_up,
        part_of(vectors[10 * model :], width),
        grad_down[:, :width],
        pick(5),
        pick(6),
        pick(7),
    )


neg_large = -1e30


def general_norm(summed, gain, bias):
    centred = summed - jnp.mean(summed, -1, keepdims=True)
    scaling = lax.rsqrt(jnp.mean(centred * centred, -1, keepdims=True) + 1e-05)
    normal_part = centred * scaling
    return (normal_part * gain + bias, normal_part, scaling)


def general_back(upstream, normal_part, scaling, gain):
    scaled = upstream * gain
    inner = (
        scaled
        - jnp.mean(scaled, -1, keepdims=True)
        - normal_part * jnp.mean(scaled * normal_part, -1, keepdims=True)
    )
    return (inner * scaling, jnp.sum(upstream * normal_part, 0), jnp.sum(upstream, 0))


def gelu_exact(inputs):
    return 0.5 * inputs * (1.0 + lax.erf(inputs * 0.7071067811865476))


def gelu_slope(inputs):
    return (
        0.5 * (1.0 + lax.erf(inputs * 0.7071067811865476))
        + inputs * jnp.exp(-0.5 * inputs * inputs) * 0.3989422804014327
    )


def general(
    layer_input,
    segments,
    w_qkv,
    b_qv,
    w_out,
    b_out,
    ln1_gain,
    ln1_bias,
    w_up,
    b_up,
    w_down,
    b_down,
    ln2_gain,
    ln2_bias,
    cotangent,
):
    inputs = layer_input[0]
    tokens = inputs.shape[0]
    group_len = tokens * lax.axis_size("ctx")
    seg_all = segments[0]
    seg_query = lax.dynamic_slice_in_dim(seg_all, lax.axis_index("ctx") * tokens, tokens)
    qkv_full, out_full, up_full, down_full = (
        lax.all_gather(w_qkv, ("shard", "ctx"), axis=0, tiled=True),
        lax.all_gather(w_out, ("shard", "ctx"), axis=0, tiled=True),
        lax.all_gather(w_up, ("shard", "ctx"), axis=0, tiled=True),
        lax.all_gather(w_down, ("shard", "ctx"), axis=0, tiled=True),
    )
    local_width = qkv_full.shape[2]
    heads_here = local_width // HD
    projected = jnp.einsum("td,dwe->wte", inputs, qkv_full, preferred_element_type=jnp.float32)
    bias_pair = b_qv.astype(jnp.float32)
    queries = (projected[0] + bias_pair[0]).astype(jnp.bfloat16)
    key_rows = projected[1].astype(jnp.bfloat16)
    value_rows = (projected[2] + bias_pair[1]).astype(jnp.bfloat16)
    keys_all, values_all = (
        lax.all_gather(key_rows, "ctx", axis=0, tiled=True),
        lax.all_gather(value_rows, "ctx", axis=0, tiled=True),
    )
    query_heads = queries.reshape(tokens, heads_here, HD).transpose(1, 0, 2)
    width_block = min(512, group_len)
    count_blocks = group_len // width_block
    key_blocks = keys_all.reshape(count_blocks, width_block, heads_here, HD)
    value_blocks = values_all.reshape(count_blocks, width_block, heads_here, HD)
    seg_blocks = seg_all.reshape(count_blocks, width_block)

    def scores_of(key_block, seg_block):
        raw = 0.125 * jnp.einsum(
            "htd,khd->htk", query_heads, key_block, preferred_element_type=jnp.float32
        )
        return jnp.where((seg_query[:, None] == seg_block[None, :])[None], raw, neg_large)

    def running_stats(carry, element):
        top_now, mass = carry
        scores = scores_of(element[0], element[1])
        top_next = jnp.maximum(top_now, jnp.max(scores, -1))
        mass = mass * jnp.exp(top_now - top_next) + jnp.sum(
            jnp.exp(scores - top_next[..., None]), -1
        )
        return ((top_next, mass), None)

    start_top = jnp.full((heads_here, tokens), neg_large, jnp.float32)
    (top_final, mass_final), unused = lax.scan(
        running_stats, (start_top, jnp.zeros_like(start_top)), (key_blocks, seg_blocks)
    )
    log_mass = top_final + jnp.log(mass_final)

    def mix_values(accum, element):
        probs = jnp.exp(scores_of(element[0], element[2]) - log_mass[..., None]).astype(
            jnp.bfloat16
        )
        return (
            accum
            + jnp.einsum("htk,khd->htd", probs, element[1], preferred_element_type=jnp.float32),
            None,
        )

    blocks_all = (key_blocks, value_blocks, seg_blocks)
    attended, unused = lax.scan(
        mix_values, jnp.zeros((heads_here, tokens, HD), jnp.float32), blocks_all
    )
    attended_rows = attended.transpose(1, 0, 2).reshape(tokens, local_width).astype(jnp.bfloat16)
    branch_part = jnp.einsum(
        "te,de->td", attended_rows, out_full, preferred_element_type=jnp.float32
    )
    branch = lax.psum(branch_part.astype(jnp.bfloat16), "tensor").astype(
        jnp.float32
    ) + b_out.astype(jnp.float32)
    first_gain = ln1_gain.astype(jnp.float32)
    second_gain = ln2_gain.astype(jnp.float32)
    hidden, first_normal, first_scale = general_norm(
        inputs.astype(jnp.float32) + branch, first_gain, ln1_bias.astype(jnp.float32)
    )
    hidden_low = hidden.astype(jnp.bfloat16)
    pre_act = jnp.dot(hidden_low, up_full, preferred_element_type=jnp.float32) + b_up.astype(
        jnp.float32
    )
    activated = gelu_exact(pre_act).astype(jnp.bfloat16)
    second_part = jnp.einsum("tf,df->td", activated, down_full, preferred_element_type=jnp.float32)
    second_branch = lax.psum(second_part.astype(jnp.bfloat16), "tensor").astype(
        jnp.float32
    ) + b_down.astype(jnp.float32)
    result, second_normal, second_scale = general_norm(
        hidden + second_branch, second_gain, ln2_bias.astype(jnp.float32)
    )
    qkv_full, out_full, up_full, down_full = (
        lax.all_gather(w_qkv, ("shard", "ctx"), axis=0, tiled=True),
        lax.all_gather(w_out, ("shard", "ctx"), axis=0, tiled=True),
        lax.all_gather(w_up, ("shard", "ctx"), axis=0, tiled=True),
        lax.all_gather(w_down, ("shard", "ctx"), axis=0, tiled=True),
    )
    upstream = cotangent[0].astype(jnp.float32)
    second_grad, grad_gain_two, grad_bias_two = general_back(
        upstream, second_normal, second_scale, second_gain
    )
    grad_down_bias = jnp.sum(second_grad, 0)
    second_low = second_grad.astype(jnp.bfloat16)
    grad_down = jnp.einsum("td,tf->df", second_low, activated, preferred_element_type=jnp.float32)
    act_grad = jnp.einsum("td,df->tf", second_low, down_full, preferred_element_type=jnp.float32)
    pre_grad = act_grad * gelu_slope(pre_act)
    grad_up_bias = jnp.sum(pre_grad, 0)
    pre_low = pre_grad.astype(jnp.bfloat16)
    grad_up = jnp.einsum("td,tf->df", hidden_low, pre_low, preferred_element_type=jnp.float32)
    hidden_part = jnp.einsum("tf,df->td", pre_low, up_full, preferred_element_type=jnp.float32)
    hidden_grad = second_grad + lax.psum(hidden_part.astype(jnp.bfloat16), "tensor").astype(
        jnp.float32
    )
    first_grad, grad_gain_one, grad_bias_one = general_back(
        hidden_grad, first_normal, first_scale, first_gain
    )
    grad_out_bias = jnp.sum(first_grad, 0)
    first_low = first_grad.astype(jnp.bfloat16)
    grad_out = jnp.einsum("td,te->de", first_low, attended_rows, preferred_element_type=jnp.float32)
    attended_grad = jnp.einsum(
        "td,de->te", first_low, out_full, preferred_element_type=jnp.float32
    ).astype(jnp.bfloat16)
    grad_heads = attended_grad.reshape(tokens, heads_here, HD).transpose(1, 0, 2)
    row_delta = jnp.sum(grad_heads.astype(jnp.float32) * attended, -1)

    def prob_pair(element):
        probs = jnp.exp(scores_of(element[0], element[2]) - log_mass[..., None])
        prob_grad = jnp.einsum(
            "htd,khd->htk", grad_heads, element[1], preferred_element_type=jnp.float32
        )
        return (probs, prob_grad)

    zero_heads = jnp.zeros((heads_here, tokens, HD), jnp.float32)

    def score_grads(accum, element):
        probs, prob_grad = prob_pair(element)
        score_grad = (probs * (prob_grad - row_delta[..., None])).astype(jnp.bfloat16)
        accum = accum + 0.125 * jnp.einsum(
            "htk,khd->htd", score_grad, element[0], preferred_element_type=jnp.float32
        )
        key_grad = 0.125 * jnp.einsum(
            "htk,htd->khd", score_grad, query_heads, preferred_element_type=jnp.float32
        )
        value_grad = jnp.einsum(
            "htk,htd->khd",
            probs.astype(jnp.bfloat16),
            grad_heads,
            preferred_element_type=jnp.float32,
        )
        return (accum, (key_grad, value_grad))

    query_grad, (key_parts, value_parts) = lax.scan(score_grads, zero_heads, blocks_all)
    key_sum, value_sum = (
        lax.psum_scatter(
            key_parts.reshape(group_len, local_width).astype(jnp.bfloat16),
            "ctx",
            scatter_dimension=0,
            tiled=True,
        ).astype(jnp.float32),
        lax.psum_scatter(
            value_parts.reshape(group_len, local_width).astype(jnp.bfloat16),
            "ctx",
            scatter_dimension=0,
            tiled=True,
        ).astype(jnp.float32),
    )
    query_rows = query_grad.transpose(1, 0, 2).reshape(tokens, local_width)
    bias_grads = jnp.stack([jnp.sum(query_rows, 0), jnp.sum(value_sum, 0)])
    stacked = jnp.stack([query_rows, key_sum, value_sum]).astype(jnp.bfloat16)
    grad_qkv = jnp.einsum("td,wte->dwe", inputs, stacked, preferred_element_type=jnp.float32)
    input_part = jnp.einsum("wte,dwe->td", stacked, qkv_full, preferred_element_type=jnp.float32)
    grad_inputs = first_grad + lax.psum(input_part.astype(jnp.bfloat16), "tensor").astype(
        jnp.float32
    )
    matrices = (
        lax.psum_scatter(grad_qkv, ("shard", "ctx"), scatter_dimension=0, tiled=True),
        lax.psum_scatter(grad_out, ("shard", "ctx"), scatter_dimension=0, tiled=True),
        lax.psum_scatter(grad_up, ("shard", "ctx"), scatter_dimension=0, tiled=True),
        lax.psum_scatter(grad_down, ("shard", "ctx"), scatter_dimension=0, tiled=True),
    )
    vectors = lax.psum(
        (
            bias_grads,
            grad_out_bias,
            grad_gain_one,
            grad_bias_one,
            grad_up_bias,
            grad_down_bias,
            grad_gain_two,
            grad_bias_two,
        ),
        ("shard", "ctx"),
    )
    return (
        result.astype(jnp.bfloat16)[None],
        grad_inputs[None],
        matrices[0],
        vectors[0],
        matrices[1],
        vectors[1],
        vectors[2],
        vectors[3],
        matrices[2],
        vectors[4],
        matrices[3],
        vectors[5],
        vectors[6],
        vectors[7],
    )


def solution(mesh):
    sizes = dict(mesh.shape)
    ctx = sizes["ctx"]
    fits = sizes["shard"] == 4 and sizes["tensor"] == 2 and ctx & (ctx - 1) == 0
    if fits:
        mesh = Mesh(mesh.devices.reshape(2, 2, ctx, 2), EVERY)
        shard, body = ("y", "core"), on_device
        rows = ("y", "core", "ctx")
    else:
        shard, body = "shard", general
        rows = ("shard", "ctx")
    activations, matrix = P(shard, "ctx", None), P(rows, "tensor")
    cube, pair = P(rows, None, "tensor"), P(None, "tensor")
    return jax.shard_map(
        body,
        mesh=mesh,
        in_specs=(
            activations, P(shard, None), cube, pair, matrix, P(), P(), P(), matrix, P("tensor"),
            matrix, P(), P(), P(), activations,
        ),
        out_specs=(
            activations, activations, cube, pair, matrix, P(), P(), P(), matrix, P("tensor"),
            matrix, P(), P(), P(),
        ),
        check_vma=False,
    )
```
